256 devices in a mesh: tm: 8 (over y, x_hi), lon: 32 (over x_lo, z, core).
Axes of the slice: x: 4 (x_hi: 2, x_lo: 2; x = x_hi * 2 + x_lo), y: 4, z: 8, core: 2. Of those that a mesh axis runs over, the one named last changes fastest.
Arguments:
- frames: bfloat16 [64, 16, 24, 4096], P(None, 'tm', None, 'lon'), may hold values from -6 to 6
- cotangent: bfloat16 [64, 16, 24, 4096], P(None, 'tm', None, 'lon'), may hold values from -6 to 6
- w_space: bfloat16 [3, 3, 64, 64], replicated, may hold values from -0.25 to 0.25
- w_time: bfloat16 [3, 64, 64], replicated, may hold values from -0.4375 to 0.4375
Outputs:
- grad_frames: bfloat16 [64, 16, 24, 4096], P(None, 'tm', None, 'lon')
- grad_space: float32 [3, 3, 64, 64], replicated
- grad_time: float32 [3, 64, 64], replicated
The draws below stay inside these ranges and needn't reach their ends.
All inputs are finite; a program needn't handle non-finite values.
Results may differ from the reference program's by a relative error of at most 0.0049.
Values may be sent and summed in bfloat16 or wider, within the bound.
No kernel may reach another device: no remote copies, remote signals or barrier semaphores. Data moves between devices by JAX's collectives and lax.ppermute only.
A program may use at most 64 MiB of HBM per device.

```python
import math
import jax
import jax.numpy as jnp
from jax import lax

C = 64
HR = 24
NF = 16
W = 4096


def level_of(own_key, extent, cuts, low, high):
    def one(position, shards_of):
        draws = jax.random.uniform(jax.random.fold_in(jax.random.fold_in(own_key, 6), position), (shards_of,), jnp.float32, low / len(cuts), high / len(cuts))
        return jnp.repeat(jnp.exp(draws), extent[position] // shards_of).reshape((-1,) + (1,) * (len(extent) - position - 1))

    gain = one(*cuts[0])
    for cut in cuts[1:]:
        gain = gain * one(*cut)
    return gain


def bell_draw(key, extent, scale, reach, shards=(), held_as=jnp.bfloat16):
    gain = level_of(key, extent, shards, -0.22, 0.18) if shards else 1.0
    values = jax.random.normal(key, extent, jnp.float32) * scale * gain
    return jnp.minimum(jnp.maximum(values, -reach), reach).astype(held_as)


def setup_inputs(seed: int = 0) -> dict:
    seeds = jax.random.split(jax.random.key(seed), 5)
    frames = bell_draw(seeds[0], (C, NF, HR, W), 1.0, 6.0, ((1, 8), (3, 32)))
    cotangent = bell_draw(seeds[1], (C, NF, HR, W), 1.0, 6.0, ((1, 8), (3, 32)))
    w_space = bell_draw(seeds[2], (3, 3, C, C), (9 * C) ** -0.5, 0.25)
    w_time = bell_draw(seeds[3], (3, C, C), (3 * C) ** -0.5, 0.4375)
    return dict(frames=frames, cotangent=cotangent, w_space=w_space, w_time=w_time)


def pad_cycle(field):
    wrapped = jnp.concatenate([field[..., -1:], field, field[..., :1]], axis=-1)
    widths = [(0, 0)] * (field.ndim - 2) + [(1, 1), (0, 0)]
    return jnp.pad(wrapped, widths)

def silu_slope(pre):
    sigmoid_value = jax.nn.sigmoid(pre)
    return sigmoid_value * (1.0 + pre * (1.0 - sigmoid_value))

def reference(frames, cotangent, w_space, w_time):
    channels, frame_total, lat_rows, lon_cols = frames.shape
    flat = lat_rows * lon_cols
    later_ext = jnp.concatenate([cotangent, jnp.zeros((channels, 2, lat_rows, lon_cols), cotangent.dtype)], axis=1)
    contract_last = (((1,), (1,)), ((), ()))
    contract_first = (((0,), (0,)), ((), ()))

    def step(carry, index):
        grad_sp, grad_tm = carry
        frame = lax.dynamic_index_in_dim(frames, index, 1, keepdims=False)
        padded = pad_cycle(frame)
        pre = jnp.zeros((channels, flat), jnp.float32)
        for i in range(3):
            for j in range(3):
                window = padded[:, i:i + lat_rows, j:j + lon_cols].reshape(channels, flat)
                pre = pre + jnp.dot(w_space[i, j], window, preferred_element_type=jnp.float32)
        act = jax.nn.silu(pre).astype(jnp.bfloat16)
        later = lax.dynamic_slice_in_dim(later_ext, index, 3, 1)
        upstream = jnp.zeros((channels, flat), jnp.float32)
        tm_terms = []
        for k in range(3):
            later_k = later[:, k].reshape(channels, flat)
            upstream = upstream + lax.dot_general(w_time[k], later_k, contract_first, preferred_element_type=jnp.float32)
            tm_terms.append(lax.dot_general(later_k, act, contract_last, preferred_element_type=jnp.float32))
        grad_tm = grad_tm + jnp.stack(tm_terms)
        dpre = (upstream * silu_slope(pre)).astype(jnp.bfloat16)
        sp_terms = []
        for i in range(3):
            for j in range(3):
                window = padded[:, i:i + lat_rows, j:j + lon_cols].reshape(channels, flat)
                sp_terms.append(lax.dot_general(dpre, window, contract_last, preferred_element_type=jnp.float32))
        grad_sp = grad_sp + jnp.stack(sp_terms).reshape(3, 3, channels, channels)
        dpad = pad_cycle(dpre.reshape(channels, lat_rows, lon_cols))
        back = jnp.zeros((channels, flat), jnp.float32)
        for i in range(3):
            for j in range(3):
                window = dpad[:, 2 - i:2 - i + lat_rows, 2 - j:2 - j + lon_cols].reshape(channels, flat)
                back = back + lax.dot_general(w_space[i, j], window, contract_first, preferred_element_type=jnp.float32)
        return ((grad_sp, grad_tm), back.astype(jnp.bfloat16).reshape(channels, lat_rows, lon_cols))
    start = (jnp.zeros((3, 3, channels, channels), jnp.float32), jnp.zeros((3, channels, channels), jnp.float32))
    (grad_sp, grad_tm), stacked = lax.scan(step, start, jnp.arange(frame_total).astype(jnp.int32))
    scale = 1.0 / math.sqrt(frame_total * lat_rows * lon_cols)
    return (jnp.moveaxis(stacked, 0, 1), grad_sp * scale, grad_tm * scale)
```

```python
import math

import jax
import jax.numpy as jnp
import numpy as np
from jax import lax
from jax.experimental import pallas as pl
from jax.experimental.pallas import tpu as pltpu
from jax.sharding import Mesh
from jax.sharding import PartitionSpec as P

AXES = ("y", "xh", "xl", "z", "c")
TM = ("y", "xh")
LON = ("xl", "z", "c")
PLANE = ("y", "xh", "xl")
LINE = ("z", "c")
F32 = jnp.float32
BF16 = jnp.bfloat16
ROWS = 8
VMEM_LIMIT = 48 * 1024 * 1024


def dot_nt(a, b):
    return lax.dot_general(a, b, (((1,), (1,)), ((), ())), preferred_element_type=F32)


def lane_taps(slab, left, right, at):
    width = slab.shape[1]
    lane = lax.broadcasted_iota(jnp.int32, slab.shape, 1)
    wide = slab.astype(F32)
    before = jnp.where(lane == 0, pltpu.roll(left, lax.rem(width - at, width), 1), pltpu.roll(wide, 1, 1))
    after = jnp.where(lane == width - 1, pltpu.roll(right, width - 1 - at, 1), pltpu.roll(wide, width - 1, 1))
    return before.astype(BF16), slab, after.astype(BF16)


def forward_kernel(x_ref, left_ref, right_ref, w_ref, x3_ref, act_ref, slope_ref, y_ref):
    frames, rows, chans, cols = x_ref.shape
    left = left_ref[...].astype(F32)
    right = right_ref[...].astype(F32)
    weight = w_ref[...]
    zero = jnp.zeros((3 * chans, cols), F32)
    y_ref[0] = zero
    y_ref[rows + 1] = zero
    for f in range(frames):

        @pl.loop(0, rows // ROWS)
        def _(g):
            wide = []
            for r in range(ROWS):
                h = g * ROWS + r
                x3 = jnp.concatenate(lane_taps(x_ref[f, h], left, right, f * rows + h), axis=0)
                x3_ref[f, h] = x3
                wide.append(x3)
            y = jnp.dot(weight, jnp.concatenate(wide, axis=1), preferred_element_type=F32)
            for r in range(ROWS):
                y_ref[g * ROWS + r + 1] = y[:, r * cols : (r + 1) * cols]

        @pl.loop(0, rows // ROWS)
        def _(g):
            for r in range(ROWS):
                h = g * ROWS + r
                pre = (
                    y_ref[h, 0:chans]
                    + y_ref[h + 1, chans : 2 * chans]
                    + y_ref[h + 2, 2 * chans : 3 * chans]
                )
                s = 1.0 / (1.0 + jnp.exp(-pre))
                act_ref[f, h] = (pre * s).astype(BF16)
                slope_ref[f, h] = s * (1.0 + pre * (1.0 - s))


def grads_kernel(c0_ref, c1_ref, c2_ref, act_ref, slope_ref, x3_ref, w_ref, base_ref,
                 d_ref, first_ref, last_ref, sum_ref, d_scr):
    rows, chans, cols = d_ref.shape
    weight = w_ref[...]
    lane = lax.broadcasted_iota(jnp.int32, (chans, cols), 1)
    d_scr[0] = jnp.zeros((chans, cols), BF16)
    d_scr[rows + 1] = jnp.zeros((chans, cols), BF16)
    first = jnp.zeros((chans, cols), F32)
    last = jnp.zeros((chans, cols), F32)
    t_sum = jnp.zeros((3 * chans, chans), F32)
    for g in range(rows // ROWS):
        hs = range(g * ROWS, (g + 1) * ROWS)
        cot = jnp.concatenate(
            [jnp.concatenate([ref[h] for h in hs], axis=1) for ref in (c0_ref, c1_ref, c2_ref)], axis=0
        )
        up = jnp.dot(weight, cot, preferred_element_type=F32)
        for r, h in enumerate(hs):
            d = (up[:, r * cols : (r + 1) * cols] * slope_ref[h]).astype(BF16)
            d_ref[h] = d
            d_scr[h + 1] = d
            wide = d.astype(F32)
            first = jnp.where(lane == h, pltpu.roll(wide, h, 1), first)
            last = jnp.where(lane == h, pltpu.roll(wide, (h + 1) % cols, 1), last)
        act = jnp.concatenate([act_ref[h] for h in hs], axis=1)
        t_sum = t_sum + dot_nt(cot, act)
    first_ref[...] = first.astype(BF16)
    last_ref[...] = last.astype(BF16)
    g_sum = jnp.zeros((3 * chans, 3 * chans), F32)
    for g in range(rows // ROWS):
        hs = range(g * ROWS, (g + 1) * ROWS)
        d3 = jnp.concatenate(
            [jnp.concatenate([d_scr[h - i + 2] for h in hs], axis=1) for i in range(3)], axis=0
        )
        x3 = jnp.concatenate([x3_ref[h] for h in hs], axis=1)
        g_sum = g_sum + dot_nt(d3, x3)
    both = jnp.concatenate([g_sum, t_sum], axis=1)
    half = both.shape[1] // 2
    sum_ref[0] = base_ref[0] + both[:, :half]
    sum_ref[1] = base_ref[1] + both[:, half:]


def back_kernel(d_ref, left_ref, right_ref, w_ref, out_ref, z_ref):
    rows, chans, cols = d_ref.shape
    left = left_ref[...].astype(F32)
    right = right_ref[...].astype(F32)
    weight = w_ref[...]
    zero = jnp.zeros((3 * chans, cols), F32)
    z_ref[0] = zero
    z_ref[rows + 1] = zero

    @pl.loop(0, rows // ROWS)
    def _(g):
        wide = []
        for r in range(ROWS):
            h = g * ROWS + r
            before, same, after = lane_taps(d_ref[h], left, right, h)
            wide.append(jnp.concatenate([after, same, before], axis=0))
        z = jnp.dot(weight, jnp.concatenate(wide, axis=1), preferred_element_type=F32)
        for r in range(ROWS):
            z_ref[g * ROWS + r + 1] = z[:, r * cols : (r + 1) * cols]

    @pl.loop(0, rows // ROWS)
    def _(g):
        for r in range(ROWS):
            h = g * ROWS + r
            out = (
                z_ref[h + 2, 0:chans]
                + z_ref[h + 1, chans : 2 * chans]
                + z_ref[h, 2 * chans : 3 * chans]
            )
            out_ref[h] = out.astype(BF16)


def in_vmem(count):
    return [pl.BlockSpec(memory_space=pltpu.VMEM)] * count


def call(kernel, args, outs, scratch, flops):
    return pl.pallas_call(
        kernel,
        out_shape=outs,
        in_specs=in_vmem(len(args)),
        out_specs=tuple(in_vmem(len(outs))),
        scratch_shapes=scratch,
        compiler_params=pltpu.CompilerParams(vmem_limit_bytes=VMEM_LIMIT),
        cost_estimate=pl.CostEstimate(flops=flops, transcendentals=0, bytes_accessed=4_000_000),
    )(*args)


def exchange(cells, axes):
    return lax.all_to_all(cells, axes, 0, 0, tiled=True)


def spread(cells, axes):
    count = lax.axis_size(axes)
    return exchange(jnp.broadcast_to(cells[None], (count,) + cells.shape), axes)


def sum_over_all(cells):
    count = lax.axis_size(PLANE)
    parts = exchange(cells.reshape(count, -1, cells.shape[-1]), PLANE).sum(0)
    parts = spread(parts, LINE).sum(0)
    return spread(parts, PLANE).reshape(cells.shape)


def edge_swap(first, last):
    count = lax.axis_size(LON)
    left = lax.ppermute(last, LON, [(i, (i + 1) % count) for i in range(count)])
    right = lax.ppermute(first, LON, [((i + 1) % count, i) for i in range(count)])
    return left, right


def body(frames, cotangent, w_space, w_time):
    chans, nf, rows, cols = frames.shape
    shape = jax.ShapeDtypeStruct
    steps = lax.axis_size(TM)
    slabs = (rows, chans, cols)
    cot = [jnp.transpose(cotangent[:, f], (1, 0, 2)) for f in range(nf)]
    cot += [lax.ppermute(c, TM, [(i, i - 1) for i in range(1, steps)]) for c in cot]

    edge = lambda w: jnp.pad(frames[:, :, :, w].reshape(chans, nf * rows), ((0, 0), (0, cols - nf * rows)))
    left, right = edge_swap(edge(0), edge(cols - 1))
    field = jnp.transpose(frames, (1, 2, 0, 3))
    w_fwd = jnp.transpose(w_space, (0, 2, 1, 3)).reshape(3 * chans, 3 * chans)
    w_bwd = jnp.transpose(w_space, (0, 3, 1, 2)).reshape(3 * chans, 3 * chans)
    w_up = jnp.transpose(w_time, (2, 0, 1)).reshape(chans, 3 * chans)
    x3, act, slope = call(
        forward_kernel,
        (field, left, right, w_fwd),
        (
            shape((nf, rows, 3 * chans, cols), BF16),
            shape((nf,) + slabs, BF16),
            shape((nf,) + slabs, F32),
        ),
        [pltpu.VMEM((rows + 2, 3 * chans, cols), F32)],
        4_000_000_000,
    )
    total = jnp.zeros((2, 3 * chans, 2 * chans), F32)
    pieces = []
    for f in range(nf):
        dpre, first, last, total = call(
            grads_kernel,
            (cot[f], cot[f + 1], cot[f + 2], act[f], slope[f], x3[f], w_up, total),
            (
                shape(slabs, BF16),
                shape((chans, cols), BF16),
                shape((chans, cols), BF16),
                shape((2, 3 * chans, 2 * chans), F32),
            ),
            [pltpu.VMEM((rows + 2, chans, cols), BF16)],
            4_000_000_000,
        )
        d_left, d_right = edge_swap(first, last)
        (out,) = call(
            back_kernel,
            (dpre, d_left, d_right, w_bwd),
            (shape(slabs, BF16),),
            [pltpu.VMEM((rows + 2, 3 * chans, cols), F32)],
            2_000_000_000,
        )
        pieces.append(jnp.transpose(out, (1, 0, 2)))
    grad_frames = jnp.stack(pieces, axis=1)
    total = sum_over_all(total.reshape(-1, 2 * chans)).reshape(2, 3 * chans, 2 * chans)
    cells = nf * steps * rows * cols * lax.axis_size(LON)
    both = jnp.concatenate([total[0], total[1]], axis=1) * (1.0 / math.sqrt(cells))
    grad_sp = jnp.transpose(both[:, : 3 * chans].reshape(3, chans, 3, chans), (0, 2, 1, 3))
    grad_tm = both[:, 3 * chans :].reshape(3, chans, chans)
    return grad_frames, grad_sp, grad_tm


def solution(mesh):
    fine = Mesh(np.asarray(mesh.devices).reshape(4, 2, 2, 8, 2), AXES)
    field = P(None, TM, None, LON)
    return jax.shard_map(
        body,
        mesh=fine,
        in_specs=(field, field, P(), P()),
        out_specs=(field, P(), P()),
        check_vma=False,
    )
```

```python
import functools
import math

import jax
import jax.numpy as jnp
import numpy as np
from jax import lax
from jax.experimental import pallas as pl
from jax.experimental.pallas import tpu as pltpu
from jax.sharding import Mesh
from jax.sharding import PartitionSpec as P

AXES = ("y", "xh", "xl", "z", "c")
TM = ("y", "xh")
LON = ("xl", "z", "c")
PLANE = ("y", "xh", "xl")
LINE = ("z", "c")
F32 = jnp.float32
BF16 = jnp.bfloat16
ROWS = 8
GAP = 32
VMEM_LIMIT = 16 * 1024 * 1024


def dot_nt(a, b):
    return lax.dot_general(a, b, (((1,), (1,)), ((), ())), preferred_element_type=F32)


def lane_of(f, h):
    return f * GAP + h


def lane_taps(slab, edge, at):
    width = slab.shape[1]
    lane = lax.broadcasted_iota(jnp.int32, slab.shape, 1)
    wide = slab.astype(F32)
    before = jnp.where(lane == 0, pltpu.roll(edge, width - at, 1), pltpu.roll(wide, 1, 1))
    after = jnp.where(lane == width - 1, pltpu.roll(edge, width // 2 - 1 - at, 1), pltpu.roll(wide, width - 1, 1))
    return before.astype(BF16), slab, after.astype(BF16)


def edge_kernel(x_ref, c0_ref, c1_ref, right_ref, left_ref, own_ref):
    frames, rows, chans, cols = x_ref.shape
    lane = lax.broadcasted_iota(jnp.int32, (chans, cols), 1)
    sums = (jnp.zeros((chans, cols), F32),) * 6
    for f, c_ref in enumerate((c0_ref, c1_ref)):

        def step(g, sums, f=f, c_ref=c_ref):
            for r in range(ROWS):
                h = g * ROWS + r
                at = lane_of(f, h)
                here, beside = lane == at, lane == at + 1
                wide = x_ref[f, h].astype(F32)
                low = pltpu.roll(wide, at, 1)
                high = pltpu.roll(wide, at + 2, 1)
                cot = c_ref[h].astype(F32)
                vals = (low, low, high, high, pltpu.roll(cot, at, 1), pltpu.roll(cot, at + 1, 1))
                masks = (here, beside, here, beside, here, here)
                sums = tuple(jnp.where(m, v, s) for m, v, s in zip(masks, vals, sums))
            return sums

        sums = lax.fori_loop(0, rows // ROWS, step, sums)
    first, second, before_last, last, cot_first, cot_last = sums
    half = cols // 2
    last = pltpu.roll(last, cols - 1, 1)
    right_ref[0:chans] = before_last.astype(BF16)
    right_ref[chans : 2 * chans] = last.astype(BF16)
    right_ref[2 * chans : 3 * chans] = cot_last.astype(BF16)
    left_ref[0:chans] = pltpu.roll(first, half, 1).astype(BF16)
    left_ref[chans : 2 * chans] = pltpu.roll(second, half - 1, 1).astype(BF16)
    left_ref[2 * chans : 3 * chans] = pltpu.roll(cot_first, half, 1).astype(BF16)
    own_ref[...] = (first + pltpu.roll(last, half, 1)).astype(BF16)


def silu_parts(pre):
    s = 1.0 / (1.0 + jnp.exp(-pre))
    return pre * s, s * (1.0 + pre * (1.0 - s))


def forward_kernel(x_ref, from_left_ref, from_right_ref, own_ref, w_ref, x3_ref, act_ref, slope_ref, edge_slope_ref, y_ref):
    frames, rows, chans, cols = x_ref.shape
    weight = w_ref[...]
    left_half = lax.broadcasted_iota(jnp.int32, (chans, cols), 1) < cols // 2
    own = own_ref[...].astype(F32)
    taps = [
        jnp.where(left_half, a.astype(F32), b.astype(F32))
        for a, b in (
            (from_left_ref[0:chans], own),
            (from_left_ref[chans : 2 * chans], from_right_ref[0:chans]),
            (own, from_right_ref[chans : 2 * chans]),
        )
    ]
    edge = taps[1]
    ye = jnp.dot(weight, jnp.concatenate(taps, axis=0).astype(BF16), preferred_element_type=F32)
    pre = (
        pltpu.roll(ye[0:chans], 1, 1)
        + ye[chans : 2 * chans]
        + pltpu.roll(ye[2 * chans : 3 * chans], cols - 1, 1)
    )
    edge_slope_ref[...] = silu_parts(pre)[1]
    zero = jnp.zeros((3 * chans, cols), F32)
    y_ref[0] = zero
    y_ref[rows + 1] = zero
    for f in range(frames):

        @pl.loop(0, rows // ROWS)
        def _(g):
            wide = []
            for r in range(ROWS):
                h = g * ROWS + r
                x3 = jnp.concatenate(lane_taps(x_ref[f, h], edge, lane_of(f, h)), axis=0)
                x3_ref[f, h] = x3
                wide.append(x3)
            y = jnp.dot(weight, jnp.concatenate(wide, axis=1), preferred_element_type=F32)
            for r in range(ROWS):
                y_ref[g * ROWS + r + 1] = y[:, r * cols : (r + 1) * cols]

        @pl.loop(0, rows // ROWS)
        def _(g):
            for r in range(ROWS):
                h = g * ROWS + r
                pre = (
                    y_ref[h, 0:chans]
                    + y_ref[h + 1, chans : 2 * chans]
                    + y_ref[h + 2, 2 * chans : 3 * chans]
                )
                act, slope = silu_parts(pre)
                act_ref[f, h] = act.astype(BF16)
                slope_ref[f, h] = slope


def grads_kernel(f, c0_ref, c1_ref, c2_ref, act_ref, slope_ref, x3_ref, w_ref, base_ref, d_ref, sum_ref, d_scr):
    rows, chans, cols = d_ref.shape
    weight = w_ref[...]
    d_scr[0] = jnp.zeros((chans, cols), BF16)
    d_scr[rows + 1] = jnp.zeros((chans, cols), BF16)
    t_sum = jnp.zeros((3 * chans, chans), F32)
    for g in range(rows // ROWS):
        hs = range(g * ROWS, (g + 1) * ROWS)
        cot = jnp.concatenate(
            [jnp.concatenate([ref[h] for h in hs], axis=1) for ref in (c0_ref, c1_ref, c2_ref)], axis=0
        )
        up = jnp.dot(weight, cot, preferred_element_type=F32)
        for r, h in enumerate(hs):
            d = (up[:, r * cols : (r + 1) * cols] * slope_ref[f, h]).astype(BF16)
            d_ref[h] = d
            d_scr[h + 1] = d
        act = jnp.concatenate([act_ref[f, h] for h in hs], axis=1)
        t_sum = t_sum + dot_nt(cot, act)
    g_sum = jnp.zeros((3 * chans, 3 * chans), F32)
    for g in range(rows // ROWS):
        hs = range(g * ROWS, (g + 1) * ROWS)
        d3 = jnp.concatenate(
            [jnp.concatenate([d_scr[h - i + 2] for h in hs], axis=1) for i in range(3)], axis=0
        )
        x3 = jnp.concatenate([x3_ref[f, h] for h in hs], axis=1)
        g_sum = g_sum + dot_nt(d3, x3)
    both = jnp.concatenate([g_sum, t_sum], axis=1)
    half = both.shape[1] // 2
    if f == 0:
        sum_ref[0] = both[:, :half]
        sum_ref[1] = both[:, half:]
    else:
        sum_ref[0] = base_ref[0] + both[:, :half]
        sum_ref[1] = base_ref[1] + both[:, half:]


def back_kernel(d0_ref, d1_ref, near_left_ref, near_right_ref, far_left_ref, far_right_ref, slope_ref, w_up_ref, w_ref,
                out0_ref, out1_ref, z_ref):
    rows, chans, cols = d0_ref.shape
    weight = w_ref[...]
    lane = lax.broadcasted_iota(jnp.int32, (chans, cols), 1)
    left_half = lane < cols // 2
    near = jnp.where(left_half, near_left_ref[...].astype(F32), near_right_ref[...].astype(F32))
    far = jnp.where(left_half, far_left_ref[...].astype(F32), far_right_ref[...].astype(F32))
    mixed = jnp.where(lane % (2 * GAP) < GAP, pltpu.roll(near, cols - GAP, 1), pltpu.roll(far, GAP, 1))
    cot = jnp.concatenate([near, mixed, far], axis=0).astype(BF16)
    up = jnp.dot(w_up_ref[...], cot, preferred_element_type=F32)
    edge = (up * slope_ref[...]).astype(BF16).astype(F32)
    zero = jnp.zeros((3 * chans, cols), F32)
    z_ref[0] = zero
    z_ref[rows + 1] = zero
    for f, (d_ref, out_ref) in enumerate(((d0_ref, out0_ref), (d1_ref, out1_ref))):

        @pl.loop(0, rows // ROWS)
        def _(g):
            wide = []
            for r in range(ROWS):
                h = g * ROWS + r
                before, same, after = lane_taps(d_ref[h], edge, lane_of(f, h))
                wide.append(jnp.concatenate([after, same, before], axis=0))
            z = jnp.dot(weight, jnp.concatenate(wide, axis=1), preferred_element_type=F32)
            for r in range(ROWS):
                z_ref[g * ROWS + r + 1] = z[:, r * cols : (r + 1) * cols]

        @pl.loop(0, rows // ROWS)
        def _(g):
            for r in range(ROWS):
                h = g * ROWS + r
                out = (
                    z_ref[h + 2, 0:chans]
                    + z_ref[h + 1, chans : 2 * chans]
                    + z_ref[h, 2 * chans : 3 * chans]
                )
                out_ref[h] = out.astype(BF16)


def finish_kernel(scale, sum_ref, space_ref, time_ref):
    taps, chans = time_ref.shape[:2]
    for i in range(taps):
        rows = slice(i * chans, (i + 1) * chans)
        low = sum_ref[0, rows, :] * scale
        high = sum_ref[1, rows, :] * scale
        space_ref[i, 0] = low[:, :chans]
        space_ref[i, 1] = low[:, chans:]
        space_ref[i, 2] = high[:, :chans]
        time_ref[i] = high[:, chans:]


def in_vmem(count):
    return [pl.BlockSpec(memory_space=pltpu.VMEM)] * count


def call(kernel, args, outs, scratch, flops):
    return pl.pallas_call(
        kernel,
        out_shape=outs,
        in_specs=in_vmem(len(args)),
        out_specs=tuple(in_vmem(len(outs))),
        scratch_shapes=scratch,
        compiler_params=pltpu.CompilerParams(vmem_limit_bytes=VMEM_LIMIT),
        cost_estimate=pl.CostEstimate(flops=flops, transcendentals=0, bytes_accessed=flops // 1000),
    )(*args)


def exchange(cells, axes):
    return lax.all_to_all(cells, axes, 0, 0, tiled=True)


def spread(cells, axes):
    count = lax.axis_size(axes)
    return exchange(jnp.broadcast_to(cells[None], (count,) + cells.shape), axes)


def sum_over_all(cells):
    count = lax.axis_size(PLANE)
    parts = exchange(cells.reshape(count, -1, cells.shape[-1]), PLANE).sum(0)
    parts = spread(parts, LINE).sum(0)
    return spread(parts, PLANE).reshape(cells.shape)


def shifted(cells, tm_step, lon_step):
    blocks, sectors = lax.axis_size(TM), lax.axis_size(LON)
    pairs = [
        ((t + tm_step) * sectors + (s + lon_step) % sectors, t * sectors + s)
        for t in range(blocks - tm_step)
        for s in range(sectors)
    ]
    return lax.ppermute(cells, TM + LON, pairs)


def body(frames, cotangent, w_space, w_time):
    chans, nf, rows, cols = frames.shape
    shape = jax.ShapeDtypeStruct
    slabs = (rows, chans, cols)
    edge = shape((chans, cols), BF16)
    edges = shape((3 * chans, cols), BF16)
    sums = shape((2, 3 * chans, 2 * chans), F32)
    cot = [jnp.transpose(cotangent[:, f], (1, 0, 2)) for f in range(nf)]
    cot[0], cot[1], frames = lax.optimization_barrier((cot[0], cot[1], frames))
    cot += [shifted(c, 1, 0) for c in cot]

    field = jnp.transpose(frames, (1, 2, 0, 3))
    to_right, to_left, own = call(edge_kernel, (field, cot[0], cot[1]), (edges, edges, edge), [], 10_000_000)
    from_left, from_right = shifted(to_right, 0, -1), shifted(to_left, 0, 1)
    far_left = shifted(to_right[2 * chans :], 1, -1)
    far_right = shifted(to_left[2 * chans :], 1, 1)
    w_fwd = jnp.transpose(w_space, (0, 2, 1, 3)).reshape(3 * chans, 3 * chans)
    w_bwd = jnp.transpose(w_space, (0, 3, 1, 2)).reshape(3 * chans, 3 * chans)
    w_up = jnp.transpose(w_time, (2, 0, 1)).reshape(chans, 3 * chans)
    x3, act, slope, edge_slope = call(
        forward_kernel,
        (field, from_left, from_right, own, w_fwd),
        (
            shape((nf, rows, 3 * chans, cols), BF16),
            shape((nf,) + slabs, BF16),
            shape((nf,) + slabs, F32),
            shape((chans, cols), F32),
        ),
        [pltpu.VMEM((rows + 2, 3 * chans, cols), F32)],
        10_000_000,
    )
    total = jnp.zeros((1, 8, 128), F32)
    dpre = []
    for f in range(nf):
        d, total = call(
            functools.partial(grads_kernel, f),
            (cot[f], cot[f + 1], cot[f + 2], act, slope, x3, w_up, total),
            (shape(slabs, BF16), sums),
            [pltpu.VMEM((rows + 2, chans, cols), BF16)],
            4_000_000_000,
        )
        dpre.append(d)
    total, far_left, far_right = lax.optimization_barrier((total, far_left, far_right))
    near = (from_left[2 * chans :], from_right[2 * chans :])
    out = call(
        back_kernel,
        (dpre[0], dpre[1], *near, far_left, far_right, edge_slope, w_up, w_bwd),
        (shape(slabs, BF16), shape(slabs, BF16)),
        [pltpu.VMEM((rows + 2, 3 * chans, cols), F32)],
        4_000_000_000,
    )
    grad_frames = jnp.stack([jnp.transpose(o, (1, 0, 2)) for o in out], axis=1)
    cells = nf * lax.axis_size(TM) * rows * cols * lax.axis_size(LON)
    total = sum_over_all(total.reshape(-1, 2 * chans)).reshape(sums.shape)
    grad_sp, grad_tm = call(
        functools.partial(finish_kernel, 1.0 / math.sqrt(cells)),
        (total,),
        (shape(w_space.shape, F32), shape(w_time.shape, F32)),
        [],
        1_000_000,
    )
    return grad_frames, grad_sp, grad_tm


def solution(mesh):
    fine = Mesh(np.asarray(mesh.devices).reshape(4, 2, 2, 8, 2), AXES)
    field = P(None, TM, None, LON)
    return jax.shard_map(
        body,
        mesh=fine,
        in_specs=(field, field, P(), P()),
        out_specs=(field, P(), P()),
        check_vma=False,
    )
```

```python
import functools
import math

import jax
import jax.numpy as jnp
import numpy as np
from jax import lax
from jax.experimental import pallas as pl
from jax.experimental.pallas import tpu as pltpu
from jax.sharding import Mesh
from jax.sharding import PartitionSpec as P

AXES = ("y", "xh", "xl", "z", "c")
TM = ("y", "xh")
LON = ("xl", "z", "c")
PLANE = ("y", "xh", "xl")
LINE = ("z", "c")
F32 = jnp.float32
BF16 = jnp.bfloat16
ROWS = 8
GAP = 32
HEAD = 12
VMEM_LIMIT = 16 * 1024 * 1024


def dot_nt(a, b):
    return lax.dot_general(a, b, (((1,), (1,)), ((), ())), preferred_element_type=F32)


def lane_of(f, h):
    return f * GAP + h


def lane_taps(slab, edge, at):
    width = slab.shape[1]
    lane = lax.broadcasted_iota(jnp.int32, slab.shape, 1)
    wide = slab.astype(F32)
    before = jnp.where(lane == 0, pltpu.roll(edge, width - at, 1), pltpu.roll(wide, 1, 1))
    after = jnp.where(lane == width - 1, pltpu.roll(edge, width // 2 - 1 - at, 1), pltpu.roll(wide, width - 1, 1))
    return before.astype(BF16), slab, after.astype(BF16)


def edge_kernel(x_ref, c0_ref, c1_ref, right_ref, left_ref, own_ref):
    frames, rows, chans, cols = x_ref.shape
    lane = lax.broadcasted_iota(jnp.int32, (chans, cols), 1)
    sums = (jnp.zeros((chans, cols), F32),) * 6
    for f, c_ref in enumerate((c0_ref, c1_ref)):

        def step(g, sums, f=f, c_ref=c_ref):
            for r in range(ROWS):
                h = g * ROWS + r
                at = lane_of(f, h)
                here, beside = lane == at, lane == at + 1
                wide = x_ref[f, h].astype(F32)
                low = pltpu.roll(wide, at, 1)
                high = pltpu.roll(wide, at + 2, 1)
                cot = c_ref[h].astype(F32)
                vals = (low, low, high, high, pltpu.roll(cot, at, 1), pltpu.roll(cot, at + 1, 1))
                masks = (here, beside, here, beside, here, here)
                sums = tuple(jnp.where(m, v, s) for m, v, s in zip(masks, vals, sums))
            return sums

        sums = lax.fori_loop(0, rows // ROWS, step, sums)
    first, second, before_last, last, cot_first, cot_last = sums
    half = cols // 2
    last = pltpu.roll(last, cols - 1, 1)
    right_ref[0:chans] = before_last.astype(BF16)
    right_ref[chans : 2 * chans] = last.astype(BF16)
    right_ref[2 * chans : 3 * chans] = cot_last.astype(BF16)
    left_ref[0:chans] = pltpu.roll(first, half, 1).astype(BF16)
    left_ref[chans : 2 * chans] = pltpu.roll(second, half - 1, 1).astype(BF16)
    left_ref[2 * chans : 3 * chans] = pltpu.roll(cot_first, half, 1).astype(BF16)
    own_ref[...] = (first + pltpu.roll(last, half, 1)).astype(BF16)


def silu_parts(pre):
    s = 1.0 / (1.0 + jnp.exp(-pre))
    return pre * s, s * (1.0 + pre * (1.0 - s))


def forward_kernel(x_ref, from_left_ref, from_right_ref, own_ref, w_ref, x3_ref, act_ref, slope_ref, edge_slope_ref, y_ref):
    frames, rows, chans, cols = x_ref.shape
    weight = w_ref[...]
    left_half = lax.broadcasted_iota(jnp.int32, (chans, cols), 1) < cols // 2
    own = own_ref[...].astype(F32)
    taps = [
        jnp.where(left_half, a.astype(F32), b.astype(F32))
        for a, b in (
            (from_left_ref[0:chans], own),
            (from_left_ref[chans : 2 * chans], from_right_ref[0:chans]),
            (own, from_right_ref[chans : 2 * chans]),
        )
    ]
    edge = taps[1]
    ye = jnp.dot(weight, jnp.concatenate(taps, axis=0).astype(BF16), preferred_element_type=F32)
    pre = (
        pltpu.roll(ye[0:chans], 1, 1)
        + ye[chans : 2 * chans]
        + pltpu.roll(ye[2 * chans : 3 * chans], cols - 1, 1)
    )
    edge_slope_ref[...] = silu_parts(pre)[1]
    zero = jnp.zeros((3 * chans, cols), F32)
    y_ref[0] = zero
    y_ref[rows + 1] = zero
    for f in range(frames):

        @pl.loop(0, rows // ROWS)
        def _(g):
            wide = []
            for r in range(ROWS):
                h = g * ROWS + r
                x3 = jnp.concatenate(lane_taps(x_ref[f, h], edge, lane_of(f, h)), axis=0)
                x3_ref[f, h] = x3
                wide.append(x3)
            y = jnp.dot(weight, jnp.concatenate(wide, axis=1), preferred_element_type=F32)
            for r in range(ROWS):
                y_ref[g * ROWS + r + 1] = y[:, r * cols : (r + 1) * cols]

        @pl.loop(0, rows // ROWS)
        def _(g):
            for r in range(ROWS):
                h = g * ROWS + r
                pre = (
                    y_ref[h, 0:chans]
                    + y_ref[h + 1, chans : 2 * chans]
                    + y_ref[h + 2, 2 * chans : 3 * chans]
                )
                act, slope = silu_parts(pre)
                act_ref[f, h] = act.astype(BF16)
                slope_ref[f, h] = slope


def grads_kernel(f, *refs):
    if f == 0:
        c0_ref, c1_ref, later_ref, act_ref, slope_ref, x3_ref, w_ref, d_ref, sum_ref, d_scr = refs
    else:
        c0_ref, c1_ref, later_ref, rest_ref, act_ref, slope_ref, x3_ref, w_ref, base_ref, d_ref, sum_ref, d_scr = refs

    def cotangent(frame, h):
        if frame < 2:
            return (c0_ref, c1_ref)[frame][h]
        at = (frame - 2) * rows + h
        return later_ref[at] if at < rows + HEAD else rest_ref[at - rows - HEAD]

    rows, chans, cols = d_ref.shape
    weight = w_ref[...]
    d_scr[0] = jnp.zeros((chans, cols), BF16)
    d_scr[rows + 1] = jnp.zeros((chans, cols), BF16)
    t_sum = jnp.zeros((3 * chans, chans), F32)
    for g in range(rows // ROWS):
        hs = range(g * ROWS, (g + 1) * ROWS)
        cot = jnp.concatenate(
            [jnp.concatenate([cotangent(f + k, h) for h in hs], axis=1) for k in range(3)], axis=0
        )
        up = jnp.dot(weight, cot, preferred_element_type=F32)
        for r, h in enumerate(hs):
            d = (up[:, r * cols : (r + 1) * cols] * slope_ref[f, h]).astype(BF16)
            d_ref[h] = d
            d_scr[h + 1] = d
        act = jnp.concatenate([act_ref[f, h] for h in hs], axis=1)
        t_sum = t_sum + dot_nt(cot, act)
    g_sum = jnp.zeros((3 * chans, 3 * chans), F32)
    for g in range(rows // ROWS):
        hs = range(g * ROWS, (g + 1) * ROWS)
        d3 = jnp.concatenate(
            [jnp.concatenate([d_scr[h - i + 2] for h in hs], axis=1) for i in range(3)], axis=0
        )
        x3 = jnp.concatenate([x3_ref[f, h] for h in hs], axis=1)
        g_sum = g_sum + dot_nt(d3, x3)
    both = jnp.concatenate([g_sum, t_sum], axis=1)
    half = both.shape[1] // 2
    if f == 0:
        sum_ref[0] = both[:, :half]
        sum_ref[1] = both[:, half:]
    else:
        sum_ref[0] = base_ref[0] + both[:, :half]
        sum_ref[1] = base_ref[1] + both[:, half:]


def back_kernel(d0_ref, d1_ref, near_ref, far_ref, slope_ref, w_up_ref, w_ref, out0_ref, out1_ref, z_ref):
    rows, chans, cols = d0_ref.shape
    weight = w_ref[...]
    lane = lax.broadcasted_iota(jnp.int32, (chans, cols), 1)
    near = near_ref[...].astype(F32)
    far = far_ref[rows - HEAD].astype(F32)
    mixed = jnp.where(lane % (2 * GAP) < GAP, pltpu.roll(near, cols - GAP, 1), pltpu.roll(far, GAP, 1))
    cot = jnp.concatenate([near, mixed, far], axis=0).astype(BF16)
    up = jnp.dot(w_up_ref[...], cot, preferred_element_type=F32)
    edge = (up * slope_ref[...]).astype(BF16).astype(F32)
    zero = jnp.zeros((3 * chans, cols), F32)
    z_ref[0] = zero
    z_ref[rows + 1] = zero
    for f, (d_ref, out_ref) in enumerate(((d0_ref, out0_ref), (d1_ref, out1_ref))):

        @pl.loop(0, rows // ROWS)
        def _(g):
            wide = []
            for r in range(ROWS):
                h = g * ROWS + r
                before, same, after = lane_taps(d_ref[h], edge, lane_of(f, h))
                wide.append(jnp.concatenate([after, same, before], axis=0))
            z = jnp.dot(weight, jnp.concatenate(wide, axis=1), preferred_element_type=F32)
            for r in range(ROWS):
                z_ref[g * ROWS + r + 1] = z[:, r * cols : (r + 1) * cols]

        @pl.loop(0, rows // ROWS)
        def _(g):
            for r in range(ROWS):
                h = g * ROWS + r
                out = (
                    z_ref[h + 2, 0:chans]
                    + z_ref[h + 1, chans : 2 * chans]
                    + z_ref[h, 2 * chans : 3 * chans]
                )
                out_ref[h] = out.astype(BF16)


def finish_kernel(scale, sum_ref, space_ref, time_ref):
    taps, chans = time_ref.shape[:2]
    for i in range(taps):
        rows = slice(i * chans, (i + 1) * chans)
        low = sum_ref[0, rows, :] * scale
        high = sum_ref[1, rows, :] * scale
        space_ref[i, 0] = low[:, :chans]
        space_ref[i, 1] = low[:, chans:]
        space_ref[i, 2] = high[:, :chans]
        time_ref[i] = high[:, chans:]


def in_vmem(count):
    return [pl.BlockSpec(memory_space=pltpu.VMEM)] * count


def call(kernel, args, outs, scratch, flops):
    return pl.pallas_call(
        kernel,
        out_shape=outs,
        in_specs=in_vmem(len(args)),
        out_specs=tuple(in_vmem(len(outs))),
        scratch_shapes=scratch,
        compiler_params=pltpu.CompilerParams(vmem_limit_bytes=VMEM_LIMIT),
        cost_estimate=pl.CostEstimate(flops=flops, transcendentals=0, bytes_accessed=flops // 1000),
    )(*args)


def exchange(cells, axes):
    return lax.all_to_all(cells, axes, 0, 0, tiled=True)


def spread(cells, axes):
    count = lax.axis_size(axes)
    return exchange(jnp.broadcast_to(cells[None], (count,) + cells.shape), axes)


def sum_over_all(cells):
    count = lax.axis_size(PLANE)
    parts = exchange(cells.reshape(count, -1, cells.shape[-1]), PLANE).sum(0)
    parts = spread(parts, LINE).sum(0)
    return spread(parts, PLANE).reshape(cells.shape)


def shifted(cells, tm_step, lon_step):
    blocks, sectors = lax.axis_size(TM), lax.axis_size(LON)
    pairs = [
        ((t + tm_step) * sectors + (s + lon_step) % sectors, t * sectors + s)
        for t in range(blocks - tm_step)
        for s in range(sectors)
    ]
    return lax.ppermute(cells, TM + LON, pairs)


def body(frames, cotangent, w_space, w_time):
    chans, nf, rows, cols = frames.shape
    shape = jax.ShapeDtypeStruct
    slabs = (rows, chans, cols)
    edge = shape((chans, cols), BF16)
    edges = shape((3 * chans, cols), BF16)
    sums = shape((2, 3 * chans, 2 * chans), F32)
    cot = [jnp.transpose(cotangent[:, f], (1, 0, 2)) for f in range(nf)]
    head = jnp.concatenate([cot[0], cot[1][:HEAD]], axis=0)
    head, frames = lax.optimization_barrier((head, frames))
    later = shifted(head, 1, 0)

    field = jnp.transpose(frames, (1, 2, 0, 3))
    to_right, to_left, own = call(edge_kernel, (field, cot[0], cot[1]), (edges, edges, edge), [], 10_000_000)
    from_left, from_right = shifted(to_right, 0, -1), shifted(to_left, 0, 1)
    near = from_left[2 * chans :] + from_right[2 * chans :]
    rest = shifted(jnp.concatenate([cot[1][HEAD:], near[None]], axis=0), 1, 0)
    w_fwd = jnp.transpose(w_space, (0, 2, 1, 3)).reshape(3 * chans, 3 * chans)
    w_bwd = jnp.transpose(w_space, (0, 3, 1, 2)).reshape(3 * chans, 3 * chans)
    w_up = jnp.transpose(w_time, (2, 0, 1)).reshape(chans, 3 * chans)
    x3, act, slope, edge_slope = call(
        forward_kernel,
        (field, from_left, from_right, own, w_fwd),
        (
            shape((nf, rows, 3 * chans, cols), BF16),
            shape((nf,) + slabs, BF16),
            shape((nf,) + slabs, F32),
            shape((chans, cols), F32),
        ),
        [pltpu.VMEM((rows + 2, 3 * chans, cols), F32)],
        10_000_000,
    )
    dpre = []
    for f in range(nf):
        d, total = call(
            functools.partial(grads_kernel, f),
            (cot[0], cot[1], later, rest, act, slope, x3, w_up, total) if f else (cot[0], cot[1], later, act, slope, x3, w_up),
            (shape(slabs, BF16), sums),
            [pltpu.VMEM((rows + 2, chans, cols), BF16)],
            4_000_000_000,
        )
        dpre.append(d)
    total, near, w_bwd = lax.optimization_barrier((total, near, w_bwd))
    out = call(
        back_kernel,
        (dpre[0], dpre[1], near, rest, edge_slope, w_up, w_bwd),
        (shape(slabs, BF16), shape(slabs, BF16)),
        [pltpu.VMEM((rows + 2, 3 * chans, cols), F32)],
        4_000_000_000,
    )
    grad_frames = jnp.stack([jnp.transpose(o, (1, 0, 2)) for o in out], axis=1)
    cells = nf * lax.axis_size(TM) * rows * cols * lax.axis_size(LON)
    total = sum_over_all(total.reshape(-1, 2 * chans)).reshape(sums.shape)
    grad_sp, grad_tm = call(
        functools.partial(finish_kernel, 1.0 / math.sqrt(cells)),
        (total,),
        (shape(w_space.shape, F32), shape(w_time.shape, F32)),
        [],
        1_000_000,
    )
    return grad_frames, grad_sp, grad_tm


def solution(mesh):
    fine = Mesh(np.asarray(mesh.devices).reshape(4, 2, 2, 8, 2), AXES)
    field = P(None, TM, None, LON)
    return jax.shard_map(
        body,
        mesh=fine,
        in_specs=(field, field, P(), P()),
        out_specs=(field, P(), P()),
        check_vma=False,
    )
```

```python
import functools
import math

import jax
import jax.numpy as jnp
import numpy as np
from jax import lax
from jax.experimental import pallas as pl
from jax.experimental.layout import Layout, with_layout_constraint
from jax.experimental.pallas import tpu as pltpu
from jax.sharding import Mesh
from jax.sharding import PartitionSpec as P

AXES = ("y", "xh", "xl", "z", "c")
TM = ("y", "xh")
LON = ("xl", "z", "c")
PLANE = ("y", "xh", "xl")
F32 = jnp.float32
BF16 = jnp.bfloat16
ROWS = 8
GAP = 32
VMEM_LIMIT = 16 * 1024 * 1024


def dot_nt(a, b):
    return lax.dot_general(a, b, (((1,), (1,)), ((), ())), preferred_element_type=F32)


def lane_of(f, h):
    return f * GAP + h


def lane_taps(slab, edge, at):
    width = slab.shape[1]
    lane = lax.broadcasted_iota(jnp.int32, slab.shape, 1)
    wide = slab.astype(F32)
    before = jnp.where(lane == 0, pltpu.roll(edge, width - at, 1), pltpu.roll(wide, 1, 1))
    after = jnp.where(lane == width - 1, pltpu.roll(edge, width // 2 - 1 - at, 1), pltpu.roll(wide, width - 1, 1))
    return before.astype(BF16), slab, after.astype(BF16)


def edge_kernel(x_ref, c_ref, right_ref, left_ref, own_ref):
    frames, rows, chans, cols = x_ref.shape
    lane = lax.broadcasted_iota(jnp.int32, (chans, cols), 1)
    sums = (jnp.zeros((chans, cols), F32),) * 6
    for f in range(frames):

        def step(g, sums, f=f):
            for r in range(ROWS):
                h = g * ROWS + r
                at = lane_of(f, h)
                here, beside = lane == at, lane == at + 1
                wide = x_ref[f, h].astype(F32)
                low = pltpu.roll(wide, at, 1)
                high = pltpu.roll(wide, at + 2, 1)
                cot = c_ref[f * rows + h].astype(F32)
                vals = (low, low, high, high, pltpu.roll(cot, at, 1), pltpu.roll(cot, at + 1, 1))
                masks = (here, beside, here, beside, here, here)
                sums = tuple(jnp.where(m, v, s) for m, v, s in zip(masks, vals, sums))
            return sums

        sums = lax.fori_loop(0, rows // ROWS, step, sums)
    first, second, before_last, last, cot_first, cot_last = sums
    half = cols // 2
    last = pltpu.roll(last, cols - 1, 1)
    right_ref[0:chans] = before_last.astype(BF16)
    right_ref[chans : 2 * chans] = last.astype(BF16)
    right_ref[2 * chans : 3 * chans] = cot_last.astype(BF16)
    left_ref[0:chans] = pltpu.roll(first, half, 1).astype(BF16)
    left_ref[chans : 2 * chans] = pltpu.roll(second, half - 1, 1).astype(BF16)
    left_ref[2 * chans : 3 * chans] = pltpu.roll(cot_first, half, 1).astype(BF16)
    own_ref[...] = (first + pltpu.roll(last, half, 1)).astype(BF16)


def silu_parts(pre):
    s = 1.0 / (1.0 + jnp.exp(-pre))
    return pre * s, s * (1.0 + pre * (1.0 - s))


def forward_kernel(x_ref, from_left_ref, from_right_ref, own_ref, w_ref, x3_ref, act_ref, slope_ref, edge_slope_ref, y_ref):
    frames, rows, chans, cols = x_ref.shape
    weight = w_ref[...]
    left_half = lax.broadcasted_iota(jnp.int32, (chans, cols), 1) < cols // 2
    own = own_ref[...].astype(F32)
    taps = [
        jnp.where(left_half, a.astype(F32), b.astype(F32))
        for a, b in (
            (from_left_ref[0:chans], own),
            (from_left_ref[chans : 2 * chans], from_right_ref[0:chans]),
            (own, from_right_ref[chans : 2 * chans]),
        )
    ]
    edge = taps[1]
    ye = jnp.dot(weight, jnp.concatenate(taps, axis=0).astype(BF16), preferred_element_type=F32)
    pre = (
        pltpu.roll(ye[0:chans], 1, 1)
        + ye[chans : 2 * chans]
        + pltpu.roll(ye[2 * chans : 3 * chans], cols - 1, 1)
    )
    edge_slope_ref[...] = silu_parts(pre)[1]
    zero = jnp.zeros((3 * chans, cols), F32)
    y_ref[0] = zero
    y_ref[rows + 1] = zero
    for f in range(frames):

        @pl.loop(0, rows // ROWS)
        def _(g):
            wide = []
            for r in range(ROWS):
                h = g * ROWS + r
                x3 = jnp.concatenate(lane_taps(x_ref[f, h], edge, lane_of(f, h)), axis=0)
                x3_ref[f, h] = x3
                wide.append(x3)
            y = jnp.dot(weight, jnp.concatenate(wide, axis=1), preferred_element_type=F32)
            for r in range(ROWS):
                y_ref[g * ROWS + r + 1] = y[:, r * cols : (r + 1) * cols]

        @pl.loop(0, rows // ROWS)
        def _(g):
            for r in range(ROWS):
                h = g * ROWS + r
                pre = (
                    y_ref[h, 0:chans]
                    + y_ref[h + 1, chans : 2 * chans]
                    + y_ref[h + 2, 2 * chans : 3 * chans]
                )
                act, slope = silu_parts(pre)
                act_ref[f, h] = act.astype(BF16)
                slope_ref[f, h] = slope


def grads_kernel(c_ref, later_ref, act_ref, slope_ref, x3_ref, w_ref, d_ref, sum_ref, d_scr):
    frames, rows, chans, cols = d_ref.shape
    weight = w_ref[...]
    t_sum = jnp.zeros((3 * chans, chans), F32)
    g_sum = jnp.zeros((3 * chans, 3 * chans), F32)
    for f in range(frames):
        d_scr[f, 0] = jnp.zeros((chans, cols), BF16)
        d_scr[f, rows + 1] = jnp.zeros((chans, cols), BF16)
        for g in range(rows // ROWS):
            hs = range(g * ROWS, (g + 1) * ROWS)
            cot = jnp.concatenate(
                [
                    jnp.concatenate([ref[at * rows + h] for h in hs], axis=1)
                    for ref, at in ((c_ref, f + k) if f + k < frames else (later_ref, f + k - frames) for k in range(3))
                ],
                axis=0,
            )
            up = jnp.dot(weight, cot, preferred_element_type=F32)
            for r, h in enumerate(hs):
                d = (up[:, r * cols : (r + 1) * cols] * slope_ref[f, h]).astype(BF16)
                d_ref[f, h] = d
                d_scr[f, h + 1] = d
            act = jnp.concatenate([act_ref[f, h] for h in hs], axis=1)
            t_sum = t_sum + dot_nt(cot, act)
        for g in range(rows // ROWS):
            hs = range(g * ROWS, (g + 1) * ROWS)
            d3 = jnp.concatenate(
                [jnp.concatenate([d_scr[f, h - i + 2] for h in hs], axis=1) for i in range(3)], axis=0
            )
            x3 = jnp.concatenate([x3_ref[f, h] for h in hs], axis=1)
            g_sum = g_sum + dot_nt(d3, x3)
    both = jnp.concatenate([g_sum, t_sum], axis=1)
    half = both.shape[1] // 2
    sum_ref[0] = both[:, :half]
    sum_ref[1] = both[:, half:]


def back_kernel(d_ref, near_ref, far_ref, slope_ref, w_up_ref, w_ref, out_ref, z_ref):
    frames, rows, chans, cols = d_ref.shape
    weight = w_ref[...]
    lane = lax.broadcasted_iota(jnp.int32, (chans, cols), 1)
    near = near_ref[...].astype(F32)
    far = far_ref[...].astype(F32)
    mixed = jnp.where(lane % (2 * GAP) < GAP, pltpu.roll(near, cols - GAP, 1), pltpu.roll(far, GAP, 1))
    cot = jnp.concatenate([near, mixed, far], axis=0).astype(BF16)
    up = jnp.dot(w_up_ref[...], cot, preferred_element_type=F32)
    edge = (up * slope_ref[...]).astype(BF16).astype(F32)
    zero = jnp.zeros((3 * chans, cols), F32)
    z_ref[0] = zero
    z_ref[rows + 1] = zero
    for f in range(frames):

        @pl.loop(0, rows // ROWS)
        def _(g):
            wide = []
            for r in range(ROWS):
                h = g * ROWS + r
                before, same, after = lane_taps(d_ref[f, h], edge, lane_of(f, h))
                wide.append(jnp.concatenate([after, same, before], axis=0))
            z = jnp.dot(weight, jnp.concatenate(wide, axis=1), preferred_element_type=F32)
            for r in range(ROWS):
                z_ref[g * ROWS + r + 1] = z[:, r * cols : (r + 1) * cols]

        @pl.loop(0, rows // ROWS)
        def _(g):
            for r in range(ROWS):
                h = g * ROWS + r
                out = (
                    z_ref[h + 2, 0:chans]
                    + z_ref[h + 1, chans : 2 * chans]
                    + z_ref[h, 2 * chans : 3 * chans]
                )
                out_ref[f, h] = out.astype(BF16)


def finish_kernel(scale, sum_ref, space_ref, time_ref):
    taps, chans = time_ref.shape[:2]
    for i in range(taps):
        rows = slice(i * chans, (i + 1) * chans)
        low = sum_ref[0, rows, :] * scale
        high = sum_ref[1, rows, :] * scale
        space_ref[i, 0] = low[:, :chans]
        space_ref[i, 1] = low[:, chans:]
        space_ref[i, 2] = high[:, :chans]
        time_ref[i] = high[:, chans:]


def in_vmem(count):
    return [pl.BlockSpec(memory_space=pltpu.VMEM)] * count


def call(kernel, args, outs, scratch, flops):
    return pl.pallas_call(
        kernel,
        out_shape=outs,
        in_specs=in_vmem(len(args)),
        out_specs=tuple(in_vmem(len(outs))),
        scratch_shapes=scratch,
        compiler_params=pltpu.CompilerParams(vmem_limit_bytes=VMEM_LIMIT),
        cost_estimate=pl.CostEstimate(flops=flops, transcendentals=0, bytes_accessed=flops // 1000),
    )(*args)


def exchange(cells, axes):
    return lax.all_to_all(cells, axes, 0, 0, tiled=True)


def spread(cells, axes):
    count = lax.axis_size(axes)
    return exchange(jnp.broadcast_to(cells[None], (count,) + cells.shape), axes)


def sum_over_all(cells, beside):
    count = lax.axis_size(PLANE)
    parts = exchange(cells.reshape(count, -1, cells.shape[-1]), PLANE)
    parts, beside = lax.optimization_barrier((parts, beside))
    parts = parts.sum(0)
    parts = parts + lax.ppermute(parts, "c", [(0, 1), (1, 0)])
    parts = spread(parts, "z").sum(0)
    return spread(parts, PLANE).reshape(cells.shape), beside


def shifted(cells, tm_step, lon_step):
    blocks, sectors = lax.axis_size(TM), lax.axis_size(LON)
    pairs = [
        ((t + tm_step) % blocks * sectors + (s + lon_step) % sectors, t * sectors + s)
        for t in range(blocks)
        for s in range(sectors)
    ]
    return lax.ppermute(cells, TM + LON, pairs)


def body(frames, cotangent, w_space, w_time):
    chans, nf, rows, cols = frames.shape
    shape = jax.ShapeDtypeStruct
    slabs = (rows, chans, cols)
    edge = shape((chans, cols), BF16)
    edges = shape((3 * chans, cols), BF16)
    sums = shape((2, 3 * chans, 2 * chans), F32)
    by_row = lambda field: jnp.transpose(field, (1, 2, 0, 3)).reshape(nf * rows, chans, cols)
    keep = (lax.axis_index(TM) < lax.axis_size(TM) - 1).astype(BF16)
    later = by_row(shifted(cotangent, 1, 0)) * keep
    cot, field = by_row(cotangent), jnp.transpose(frames, (1, 2, 0, 3))
    to_right, to_left, own = call(edge_kernel, (field, cot), (edges, edges, edge), [], 10_000_000)
    from_left, from_right = shifted(to_right, 0, -1), shifted(to_left, 0, 1)
    near = from_left[2 * chans :] + from_right[2 * chans :]
    far = shifted(near, 1, 0) * keep
    w_fwd = jnp.transpose(w_space, (0, 2, 1, 3)).reshape(3 * chans, 3 * chans)
    w_bwd = jnp.transpose(w_space, (0, 3, 1, 2)).reshape(3 * chans, 3 * chans)
    w_up = jnp.transpose(w_time, (2, 0, 1)).reshape(chans, 3 * chans)
    x3, act, slope, edge_slope = call(
        forward_kernel,
        (field, from_left, from_right, own, w_fwd),
        (
            shape((nf, rows, 3 * chans, cols), BF16),
            shape((nf,) + slabs, BF16),
            shape((nf,) + slabs, F32),
            shape((chans, cols), F32),
        ),
        [pltpu.VMEM((rows + 2, 3 * chans, cols), F32)],
        10_000_000,
    )
    dpre, total = call(
        grads_kernel,
        (cot, later, act, slope, x3, w_up),
        (shape((nf,) + slabs, BF16), sums),
        [pltpu.VMEM((nf, rows + 2, chans, cols), BF16)],
        4_000_000_000,
    )
    total, near, far, w_bwd = lax.optimization_barrier((total, near, far, w_bwd))
    (out,) = call(
        back_kernel,
        (dpre, near, far, edge_slope, w_up, w_bwd),
        (shape((nf,) + slabs, BF16),),
        [pltpu.VMEM((rows + 2, 3 * chans, cols), F32)],
        4_000_000_000,
    )
    grad_frames = with_layout_constraint(jnp.transpose(out, (2, 0, 1, 3)), Layout(major_to_minor=(0, 1, 2, 3)))
    cells = nf * lax.axis_size(TM) * rows * cols * lax.axis_size(LON)
    total, grad_frames = sum_over_all(total.reshape(-1, 2 * chans), grad_frames)
    total = total.reshape(sums.shape)
    grad_sp, grad_tm = call(
        functools.partial(finish_kernel, 1.0 / math.sqrt(cells)),
        (total,),
        (shape(w_space.shape, F32), shape(w_time.shape, F32)),
        [],
        1_000_000,
    )
    return grad_frames, grad_sp, grad_tm


def solution(mesh):
    fine = Mesh(np.asarray(mesh.devices).reshape(4, 2, 2, 8, 2), AXES)
    field = P(None, TM, None, LON)
    return jax.shard_map(
        body,
        mesh=fine,
        in_specs=(field, field, P(), P()),
        out_specs=(field, P(), P()),
        check_vma=False,
    )
```

```python
import functools
import math

import jax
import jax.numpy as jnp
import numpy as np
from jax import lax
from jax.experimental import pallas as pl
from jax.experimental.layout import Layout, with_layout_constraint
from jax.experimental.pallas import tpu as pltpu
from jax.sharding import Mesh
from jax.sharding import PartitionSpec as P

AXES = ("y", "xh", "xl", "z", "c")
TM = ("y", "xh")
LON = ("xl", "z", "c")
PLANE = ("y", "xh", "xl")
F32 = jnp.float32
BF16 = jnp.bfloat16
ROWS = 8
GAP = 32
VMEM_LIMIT = 16 * 1024 * 1024


def dot_nt(a, b):
    return lax.dot_general(a, b, (((1,), (1,)), ((), ())), preferred_element_type=F32)


def lane_of(f, h):
    return f * GAP + h


def lane_taps(slab, edge, at):
    width = slab.shape[1]
    lane = lax.broadcasted_iota(jnp.int32, slab.shape, 1)
    wide = slab.astype(F32)
    before = jnp.where(lane == 0, pltpu.roll(edge, width - at, 1), pltpu.roll(wide, 1, 1))
    after = jnp.where(lane == width - 1, pltpu.roll(edge, width // 2 - 1 - at, 1), pltpu.roll(wide, width - 1, 1))
    return before.astype(BF16), slab, after.astype(BF16)


def edge_kernel(x_ref, c_ref, right_ref, left_ref, own_ref):
    frames, rows, chans, cols = x_ref.shape
    lane = lax.broadcasted_iota(jnp.int32, (chans, cols), 1)
    sums = (jnp.zeros((chans, cols), F32),) * 6
    for f in range(frames):

        def step(g, sums, f=f):
            for r in range(ROWS):
                h = g * ROWS + r
                at = lane_of(f, h)
                here, beside = lane == at, lane == at + 1
                wide = x_ref[f, h].astype(F32)
                low = pltpu.roll(wide, at, 1)
                high = pltpu.roll(wide, at + 2, 1)
                cot = c_ref[f * rows + h].astype(F32)
                vals = (low, low, high, high, pltpu.roll(cot, at, 1), pltpu.roll(cot, at + 1, 1))
                masks = (here, beside, here, beside, here, here)
                sums = tuple(jnp.where(m, v, s) for m, v, s in zip(masks, vals, sums))
            return sums

        sums = lax.fori_loop(0, rows // ROWS, step, sums)
    first, second, before_last, last, cot_first, cot_last = sums
    half = cols // 2
    last = pltpu.roll(last, cols - 1, 1)
    right_ref[0:chans] = before_last.astype(BF16)
    right_ref[chans : 2 * chans] = last.astype(BF16)
    right_ref[2 * chans : 3 * chans] = cot_last.astype(BF16)
    left_ref[0:chans] = pltpu.roll(first, half, 1).astype(BF16)
    left_ref[chans : 2 * chans] = pltpu.roll(second, half - 1, 1).astype(BF16)
    left_ref[2 * chans : 3 * chans] = pltpu.roll(cot_first, half, 1).astype(BF16)
    own_ref[...] = (first + pltpu.roll(last, half, 1)).astype(BF16)


def silu_parts(pre):
    s = 1.0 / (1.0 + jnp.exp(-pre))
    return pre * s, s * (1.0 + pre * (1.0 - s))


def forward_kernel(x_ref, from_left_ref, from_right_ref, own_ref, w_ref, x3_ref, act_ref, slope_ref, edge_slope_ref, y_ref):
    frames, rows, chans, cols = x_ref.shape
    weight = w_ref[...]
    left_half = lax.broadcasted_iota(jnp.int32, (chans, cols), 1) < cols // 2
    own = own_ref[...].astype(F32)
    taps = [
        jnp.where(left_half, a.astype(F32), b.astype(F32))
        for a, b in (
            (from_left_ref[0:chans], own),
            (from_left_ref[chans : 2 * chans], from_right_ref[0:chans]),
            (own, from_right_ref[chans : 2 * chans]),
        )
    ]
    edge = taps[1]
    ye = jnp.dot(weight, jnp.concatenate(taps, axis=0).astype(BF16), preferred_element_type=F32)
    pre = (
        pltpu.roll(ye[0:chans], 1, 1)
        + ye[chans : 2 * chans]
        + pltpu.roll(ye[2 * chans : 3 * chans], cols - 1, 1)
    )
    edge_slope_ref[...] = silu_parts(pre)[1]
    zero = jnp.zeros((3 * chans, cols), F32)
    y_ref[0] = zero
    y_ref[rows + 1] = zero
    for f in range(frames):

        @pl.loop(0, rows // ROWS)
        def _(g):
            wide = []
            for r in range(ROWS):
                h = g * ROWS + r
                x3 = jnp.concatenate(lane_taps(x_ref[f, h], edge, lane_of(f, h)), axis=0)
                x3_ref[f, h] = x3
                wide.append(x3)
            y = jnp.dot(weight, jnp.concatenate(wide, axis=1), preferred_element_type=F32)
            for r in range(ROWS):
                y_ref[g * ROWS + r + 1] = y[:, r * cols : (r + 1) * cols]

        @pl.loop(0, rows // ROWS)
        def _(g):
            for r in range(ROWS):
                h = g * ROWS + r
                pre = (
                    y_ref[h, 0:chans]
                    + y_ref[h + 1, chans : 2 * chans]
                    + y_ref[h + 2, 2 * chans : 3 * chans]
                )
                act, slope = silu_parts(pre)
                act_ref[f, h] = act.astype(BF16)
                slope_ref[f, h] = slope


def grads_kernel(c_ref, later_ref, act_ref, slope_ref, x3_ref, w_ref, d_ref, sum_ref, d_scr):
    frames, rows, chans, cols = d_ref.shape
    weight = w_ref[...]
    wide = lambda ref, f, hs: jnp.concatenate([ref[f, h] for h in hs], axis=1)
    for f in range(frames):
        d_scr[f, 0] = jnp.zeros((chans, cols), BF16)
        d_scr[f, rows + 1] = jnp.zeros((chans, cols), BF16)
    t_sum = jnp.zeros((2 * frames * chans, frames * chans), F32)
    for g in range(rows // ROWS):
        hs = range(g * ROWS, (g + 1) * ROWS)
        cot = jnp.concatenate(
            [
                jnp.concatenate([ref[f * rows + h] for h in hs], axis=1)
                for ref in (c_ref, later_ref)
                for f in range(frames)
            ],
            axis=0,
        )
        up = jnp.dot(weight, cot, preferred_element_type=F32)
        for f in range(frames):
            for r, h in enumerate(hs):
                d = (up[f * chans : (f + 1) * chans, r * cols : (r + 1) * cols] * slope_ref[f, h]).astype(BF16)
                d_ref[f, h] = d
                d_scr[f, h + 1] = d
        t_sum = t_sum + dot_nt(cot, jnp.concatenate([wide(act_ref, f, hs) for f in range(frames)], axis=0))
    g_sum = jnp.zeros((3 * chans, 3 * chans), F32)
    for f in range(frames):
        for g in range(rows // ROWS):
            hs = range(g * ROWS, (g + 1) * ROWS)
            d3 = jnp.concatenate(
                [jnp.concatenate([d_scr[f, h - i + 2] for h in hs], axis=1) for i in range(3)], axis=0
            )
            g_sum = g_sum + dot_nt(d3, wide(x3_ref, f, hs))
    t_sum = t_sum[: 3 * chans, :chans] + t_sum[chans:, chans:]
    both = jnp.concatenate([g_sum, t_sum], axis=1)
    half = both.shape[1] // 2
    sum_ref[0] = both[:, :half]
    sum_ref[1] = both[:, half:]


def back_kernel(d_ref, near_ref, far_ref, slope_ref, w_up_ref, w_ref, out_ref, z_ref):
    frames, rows, chans, cols = d_ref.shape
    weight = w_ref[...]
    lane = lax.broadcasted_iota(jnp.int32, (chans, cols), 1)
    near = near_ref[...].astype(F32)
    far = far_ref[...].astype(F32)
    mixed = jnp.where(lane % (2 * GAP) < GAP, pltpu.roll(near, cols - GAP, 1), pltpu.roll(far, GAP, 1))
    cot = jnp.concatenate([near, mixed, far], axis=0).astype(BF16)
    up = jnp.dot(w_up_ref[...], cot, preferred_element_type=F32)
    edge = (up * slope_ref[...]).astype(BF16).astype(F32)
    zero = jnp.zeros((3 * chans, cols), F32)
    z_ref[0] = zero
    z_ref[rows + 1] = zero
    for f in range(frames):

        @pl.loop(0, rows // ROWS)
        def _(g):
            wide = []
            for r in range(ROWS):
                h = g * ROWS + r
                before, same, after = lane_taps(d_ref[f, h], edge, lane_of(f, h))
                wide.append(jnp.concatenate([after, same, before], axis=0))
            z = jnp.dot(weight, jnp.concatenate(wide, axis=1), preferred_element_type=F32)
            for r in range(ROWS):
                z_ref[g * ROWS + r + 1] = z[:, r * cols : (r + 1) * cols]

        @pl.loop(0, rows // ROWS)
        def _(g):
            for r in range(ROWS):
                h = g * ROWS + r
                out = (
                    z_ref[h + 2, 0:chans]
                    + z_ref[h + 1, chans : 2 * chans]
                    + z_ref[h, 2 * chans : 3 * chans]
                )
                out_ref[f, h] = out.astype(BF16)


def finish_kernel(scale, sum_ref, space_ref, time_ref):
    taps, chans = time_ref.shape[:2]
    for i in range(taps):
        rows = slice(i * chans, (i + 1) * chans)
        low = sum_ref[0, rows, :].astype(F32) * scale
        high = sum_ref[1, rows, :].astype(F32) * scale
        space_ref[i, 0] = low[:, :chans]
        space_ref[i, 1] = low[:, chans:]
        space_ref[i, 2] = high[:, :chans]
        time_ref[i] = high[:, chans:]


def in_vmem(count):
    return [pl.BlockSpec(memory_space=pltpu.VMEM)] * count


def call(kernel, args, outs, scratch, flops):
    return pl.pallas_call(
        kernel,
        out_shape=outs,
        in_specs=in_vmem(len(args)),
        out_specs=tuple(in_vmem(len(outs))),
        scratch_shapes=scratch,
        compiler_params=pltpu.CompilerParams(vmem_limit_bytes=VMEM_LIMIT),
        cost_estimate=pl.CostEstimate(flops=flops, transcendentals=0, bytes_accessed=flops // 1000),
    )(*args)


def exchange(cells, axes):
    return lax.all_to_all(cells, axes, 0, 0, tiled=True)


def spread(cells, axes):
    count = lax.axis_size(axes)
    return exchange(jnp.broadcast_to(cells[None], (count,) + cells.shape), axes)


def sum_over_all(cells, beside):
    count = lax.axis_size(PLANE)
    parts = exchange(cells.reshape(count, -1, cells.shape[-1]), PLANE)
    parts, beside = lax.optimization_barrier((parts, beside))
    parts = parts.sum(0)
    parts = parts + lax.ppermute(parts, "c", [(0, 1), (1, 0)])
    parts = spread(parts, "z").sum(0)
    return spread(parts.astype(BF16), PLANE).reshape(cells.shape), beside


def shifted(cells, tm_step, lon_step):
    blocks, sectors = lax.axis_size(TM), lax.axis_size(LON)
    pairs = [
        ((t + tm_step) % blocks * sectors + (s + lon_step) % sectors, t * sectors + s)
        for t in range(blocks)
        for s in range(sectors)
    ]
    return lax.ppermute(cells, TM + LON, pairs)


def body(frames, cotangent, w_space, w_time):
    chans, nf, rows, cols = frames.shape
    shape = jax.ShapeDtypeStruct
    slabs = (rows, chans, cols)
    edge = shape((chans, cols), BF16)
    edges = shape((3 * chans, cols), BF16)
    sums = shape((2, 3 * chans, 2 * chans), F32)
    by_row = lambda field: jnp.transpose(field, (1, 2, 0, 3)).reshape(nf * rows, chans, cols)
    keep = (lax.axis_index(TM) < lax.axis_size(TM) - 1).astype(BF16)
    later = by_row(shifted(cotangent, 1, 0)) * keep
    cot, field = by_row(cotangent), jnp.transpose(frames, (1, 2, 0, 3))
    to_right, to_left, own = call(edge_kernel, (field, cot), (edges, edges, edge), [], 10_000_000)
    from_left, from_right = shifted(to_right, 0, -1), shifted(to_left, 0, 1)
    near = from_left[2 * chans :] + from_right[2 * chans :]
    far = shifted(near, 1, 0) * keep
    w_fwd = jnp.transpose(w_space, (0, 2, 1, 3)).reshape(3 * chans, 3 * chans)
    w_bwd = jnp.transpose(w_space, (0, 3, 1, 2)).reshape(3 * chans, 3 * chans)
    w_up = jnp.transpose(w_time, (2, 0, 1)).reshape(chans, 3 * chans)
    w_both = jnp.concatenate([jnp.pad(w_up, ((0, 0), (f * chans, (nf - 1 - f) * chans))) for f in range(nf)], axis=0)
    x3, act, slope, edge_slope = call(
        forward_kernel,
        (field, from_left, from_right, own, w_fwd),
        (
            shape((nf, rows, 3 * chans, cols), BF16),
            shape((nf,) + slabs, BF16),
            shape((nf,) + slabs, F32),
            shape((chans, cols), F32),
        ),
        [pltpu.VMEM((rows + 2, 3 * chans, cols), F32)],
        10_000_000,
    )
    dpre, total = call(
        grads_kernel,
        (cot, later, act, slope, x3, w_both),
        (shape((nf,) + slabs, BF16), sums),
        [pltpu.VMEM((nf, rows + 2, chans, cols), BF16)],
        4_000_000_000,
    )
    total, near, far, w_bwd = lax.optimization_barrier((total, near, far, w_bwd))
    (out,) = call(
        back_kernel,
        (dpre, near, far, edge_slope, w_up, w_bwd),
        (shape((nf,) + slabs, BF16),),
        [pltpu.VMEM((rows + 2, 3 * chans, cols), F32)],
        4_000_000_000,
    )
    grad_frames = with_layout_constraint(jnp.transpose(out, (2, 0, 1, 3)), Layout(major_to_minor=(0, 1, 2, 3)))
    cells = nf * lax.axis_size(TM) * rows * cols * lax.axis_size(LON)
    total, grad_frames = sum_over_all(total.reshape(-1, 2 * chans), grad_frames)
    total = total.reshape(sums.shape)
    grad_sp, grad_tm = call(
        functools.partial(finish_kernel, 1.0 / math.sqrt(cells)),
        (total,),
        (shape(w_space.shape, F32), shape(w_time.shape, F32)),
        [],
        1_000_000,
    )
    return grad_frames, grad_sp, grad_tm


def solution(mesh):
    fine = Mesh(np.asarray(mesh.devices).reshape(4, 2, 2, 8, 2), AXES)
    field = P(None, TM, None, LON)
    return jax.shard_map(
        body,
        mesh=fine,
        in_specs=(field, field, P(), P()),
        out_specs=(field, P(), P()),
        check_vma=False,
    )
```

```python
import functools
import math

import jax
import jax.numpy as jnp
import numpy as np
from jax import lax
from jax.experimental import pallas as pl
from jax.experimental.layout import Layout, with_layout_constraint
from jax.experimental.pallas import tpu as pltpu
from jax.sharding import Mesh
from jax.sharding import PartitionSpec as P

AXES = ("y", "xh", "xl", "z", "c")
TM = ("y", "xh")
LON = ("xl", "z", "c")
PLANE = ("y", "xh", "xl")
F32 = jnp.float32
BF16 = jnp.bfloat16
ROWS = 8
GAP = 32
VMEM_LIMIT = 16 * 1024 * 1024


def dot_nt(a, b):
    return lax.dot_general(a, b, (((1,), (1,)), ((), ())), preferred_element_type=F32)


def lane_of(f, h):
    return f * GAP + h


def lane_taps(slab, edge, at):
    width = slab.shape[1]
    lane = lax.broadcasted_iota(jnp.int32, slab.shape, 1)
    wide = slab.astype(F32)
    before = jnp.where(lane == 0, pltpu.roll(edge, lax.rem(width - at, width), 1), pltpu.roll(wide, 1, 1))
    after = jnp.where(lane == width - 1, pltpu.roll(edge, width // 2 - 1 - at, 1), pltpu.roll(wide, width - 1, 1))
    return before.astype(BF16), slab, after.astype(BF16)


def edge_kernel(x_ref, c_ref, right_ref, left_ref, own_ref):
    frames, rows, chans, cols = x_ref.shape
    lane = lax.broadcasted_iota(jnp.int32, (chans, cols), 1)
    sums = (jnp.zeros((chans, cols), F32),) * 6
    for f in range(frames):

        def step(g, sums, f=f):
            for r in range(ROWS):
                h = g * ROWS + r
                at = lane_of(f, h)
                here, beside = lane == at, lane == at + 1
                wide = x_ref[f, h].astype(F32)
                low = pltpu.roll(wide, at, 1)
                high = pltpu.roll(wide, at + 2, 1)
                cot = c_ref[f * rows + h].astype(F32)
                vals = (low, low, high, high, pltpu.roll(cot, at, 1), pltpu.roll(cot, at + 1, 1))
                masks = (here, beside, here, beside, here, here)
                sums = tuple(jnp.where(m, v, s) for m, v, s in zip(masks, vals, sums))
            return sums

        sums = lax.fori_loop(0, rows // ROWS, step, sums)
    first, second, before_last, last, cot_first, cot_last = sums
    half = cols // 2
    last = pltpu.roll(last, cols - 1, 1)
    right_ref[0:chans] = before_last.astype(BF16)
    right_ref[chans : 2 * chans] = last.astype(BF16)
    right_ref[2 * chans : 3 * chans] = cot_last.astype(BF16)
    left_ref[0:chans] = pltpu.roll(first, half, 1).astype(BF16)
    left_ref[chans : 2 * chans] = pltpu.roll(second, half - 1, 1).astype(BF16)
    left_ref[2 * chans : 3 * chans] = pltpu.roll(cot_first, half, 1).astype(BF16)
    own_ref[...] = (first + pltpu.roll(last, half, 1)).astype(BF16)


def silu_parts(pre):
    s = 1.0 / (1.0 + jnp.exp(-pre))
    return pre * s, s * (1.0 + pre * (1.0 - s))


def forward_kernel(x_ref, from_left_ref, from_right_ref, own_ref, w_ref, x3_ref, act_ref, slope_ref, edge_slope_ref, y_ref):
    frames, rows, chans, cols = x_ref.shape
    weight = w_ref[...]
    left_half = lax.broadcasted_iota(jnp.int32, (chans, cols), 1) < cols // 2
    own = own_ref[...].astype(F32)
    taps = [
        jnp.where(left_half, a.astype(F32), b.astype(F32))
        for a, b in (
            (from_left_ref[0:chans], own),
            (from_left_ref[chans : 2 * chans], from_right_ref[0:chans]),
            (own, from_right_ref[chans : 2 * chans]),
        )
    ]
    edge = taps[1]
    ye = jnp.dot(weight, jnp.concatenate(taps, axis=0).astype(BF16), preferred_element_type=F32)
    pre = (
        pltpu.roll(ye[0:chans], 1, 1)
        + ye[chans : 2 * chans]
        + pltpu.roll(ye[2 * chans : 3 * chans], cols - 1, 1)
    )
    edge_slope_ref[...] = silu_parts(pre)[1]
    zero = jnp.zeros((3 * chans, cols), F32)
    y_ref[0] = zero
    y_ref[rows + 1] = zero
    for f in range(frames):

        @pl.loop(0, rows // ROWS)
        def _(g):
            wide = []
            for r in range(ROWS):
                h = g * ROWS + r
                x3 = jnp.concatenate(lane_taps(x_ref[f, h], edge, lane_of(f, h)), axis=0)
                x3_ref[f, h] = x3
                wide.append(x3)
            y = jnp.dot(weight, jnp.concatenate(wide, axis=1), preferred_element_type=F32)
            for r in range(ROWS):
                y_ref[g * ROWS + r + 1] = y[:, r * cols : (r + 1) * cols]

        @pl.loop(0, rows // ROWS)
        def _(g):
            for r in range(ROWS):
                h = g * ROWS + r
                pre = (
                    y_ref[h, 0:chans]
                    + y_ref[h + 1, chans : 2 * chans]
                    + y_ref[h + 2, 2 * chans : 3 * chans]
                )
                act, slope = silu_parts(pre)
                act_ref[f, h] = act.astype(BF16)
                slope_ref[f, h] = slope


def grads_kernel(c_ref, later_ref, act_ref, slope_ref, x3_ref, w_ref, d_ref, sum_ref, d_scr):
    frames, rows, chans, cols = d_ref.shape
    weight = w_ref[...]
    wide = lambda ref, f, hs: jnp.concatenate([ref[f, h] for h in hs], axis=1)
    for f in range(frames):
        d_scr[f, 0] = jnp.zeros((chans, cols), BF16)
        d_scr[f, rows + 1] = jnp.zeros((chans, cols), BF16)
    t_sum = jnp.zeros((2 * frames * chans, frames * chans), F32)
    for g in range(rows // ROWS):
        hs = range(g * ROWS, (g + 1) * ROWS)
        cot = jnp.concatenate(
            [
                jnp.concatenate([ref[f * rows + h] for h in hs], axis=1)
                for ref in (c_ref, later_ref)
                for f in range(frames)
            ],
            axis=0,
        )
        up = jnp.dot(weight, cot, preferred_element_type=F32)
        for f in range(frames):
            for r, h in enumerate(hs):
                d = (up[f * chans : (f + 1) * chans, r * cols : (r + 1) * cols] * slope_ref[f, h]).astype(BF16)
                d_ref[f, h] = d
                d_scr[f, h + 1] = d
        t_sum = t_sum + dot_nt(cot, jnp.concatenate([wide(act_ref, f, hs) for f in range(frames)], axis=0))
    g_sum = jnp.zeros((3 * chans, 3 * chans), F32)
    for f in range(frames):
        for g in range(rows // ROWS):
            hs = range(g * ROWS, (g + 1) * ROWS)
            d3 = jnp.concatenate(
                [jnp.concatenate([d_scr[f, h - i + 2] for h in hs], axis=1) for i in range(3)], axis=0
            )
            g_sum = g_sum + dot_nt(d3, wide(x3_ref, f, hs))
    t_sum = t_sum[: 3 * chans, :chans] + t_sum[chans:, chans:]
    both = jnp.concatenate([g_sum, t_sum], axis=1)
    half = both.shape[1] // 2
    sum_ref[0] = both[:, :half]
    sum_ref[1] = both[:, half:]


def back_kernel(d_ref, near_ref, far_ref, slope_ref, w_up_ref, w_ref, out_ref, z_ref):
    frames, rows, chans, cols = d_ref.shape
    weight = w_ref[...]
    lane = lax.broadcasted_iota(jnp.int32, (chans, cols), 1)
    near = near_ref[...].astype(F32)
    far = far_ref[...].astype(F32)
    mixed = jnp.where(lane % (2 * GAP) < GAP, pltpu.roll(near, cols - GAP, 1), pltpu.roll(far, GAP, 1))
    cot = jnp.concatenate([near, mixed, far], axis=0).astype(BF16)
    up = jnp.dot(w_up_ref[...], cot, preferred_element_type=F32)
    edge = (up * slope_ref[...]).astype(BF16).astype(F32)
    zero = jnp.zeros((3 * chans, cols), F32)
    z_ref[0] = zero
    z_ref[rows + 1] = zero
    for f in range(frames):

        @pl.loop(0, rows // ROWS)
        def _(g):
            wide = []
            for r in range(ROWS):
                h = g * ROWS + r
                before, same, after = lane_taps(d_ref[f, h], edge, lane_of(f, h))
                wide.append(jnp.concatenate([after, same, before], axis=0))
            z = jnp.dot(weight, jnp.concatenate(wide, axis=1), preferred_element_type=F32)
            for r in range(ROWS):
                z_ref[g * ROWS + r + 1] = z[:, r * cols : (r + 1) * cols]

        @pl.loop(0, rows // ROWS)
        def _(g):
            for r in range(ROWS):
                h = g * ROWS + r
                out = (
                    z_ref[h + 2, 0:chans]
                    + z_ref[h + 1, chans : 2 * chans]
                    + z_ref[h, 2 * chans : 3 * chans]
                )
                out_ref[f, h] = out.astype(BF16)


def finish_kernel(scale, sum_ref, space_ref, time_ref):
    taps, chans = time_ref.shape[:2]
    for i in range(taps):
        rows = slice(i * chans, (i + 1) * chans)
        low = sum_ref[0, rows, :].astype(F32) * scale
        high = sum_ref[1, rows, :].astype(F32) * scale
        space_ref[i, 0] = low[:, :chans]
        space_ref[i, 1] = low[:, chans:]
        space_ref[i, 2] = high[:, :chans]
        time_ref[i] = high[:, chans:]


def in_vmem(count):
    return [pl.BlockSpec(memory_space=pltpu.VMEM)] * count


def call(kernel, args, outs, scratch, flops):
    return pl.pallas_call(
        kernel,
        out_shape=outs,
        in_specs=in_vmem(len(args)),
        out_specs=tuple(in_vmem(len(outs))),
        scratch_shapes=scratch,
        compiler_params=pltpu.CompilerParams(vmem_limit_bytes=VMEM_LIMIT),
        cost_estimate=pl.CostEstimate(flops=flops, transcendentals=0, bytes_accessed=flops // 1000),
    )(*args)


def exchange(cells, axes):
    return lax.all_to_all(cells, axes, 0, 0, tiled=True)


def spread(cells, axes):
    count = lax.axis_size(axes)
    return exchange(jnp.broadcast_to(cells[None], (count,) + cells.shape), axes)


def sum_over_all(cells, beside):
    count = lax.axis_size(PLANE)
    parts = exchange(cells.reshape(count, -1, cells.shape[-1]), PLANE)
    parts, beside = lax.optimization_barrier((parts, beside))
    parts = parts.sum(0)
    parts = parts + lax.ppermute(parts, "c", [(0, 1), (1, 0)])
    parts = spread(parts, "z").sum(0)
    return spread(parts.astype(BF16), PLANE).reshape(cells.shape), beside


def shifted(cells, tm_step, lon_step):
    blocks, sectors = lax.axis_size(TM), lax.axis_size(LON)
    pairs = [
        ((t + tm_step) % blocks * sectors + (s + lon_step) % sectors, t * sectors + s)
        for t in range(blocks)
        for s in range(sectors)
    ]
    return lax.ppermute(cells, TM + LON, pairs)


def body(frames, cotangent, w_space, w_time):
    chans, nf, rows, cols = frames.shape
    shape = jax.ShapeDtypeStruct
    slabs = (rows, chans, cols)
    edge = shape((chans, cols), BF16)
    edges = shape((3 * chans, cols), BF16)
    sums = shape((2, 3 * chans, 2 * chans), F32)
    by_row = lambda field: jnp.transpose(field, (1, 2, 0, 3)).reshape(nf * rows, chans, cols)
    keep = (lax.axis_index(TM) < lax.axis_size(TM) - 1).astype(BF16)
    later = by_row(shifted(cotangent, 1, 0)) * keep
    cot, field = by_row(cotangent), jnp.transpose(frames, (1, 2, 0, 3))
    to_right, to_left, own = call(edge_kernel, (field, cot), (edges, edges, edge), [], 10_000_000)
    from_left, from_right = shifted(to_right, 0, -1), shifted(to_left, 0, 1)
    near = from_left[2 * chans :] + from_right[2 * chans :]
    far = shifted(near, 1, 0) * keep
    w_fwd = jnp.transpose(w_space, (0, 2, 1, 3)).reshape(3 * chans, 3 * chans)
    w_bwd = jnp.transpose(w_space, (0, 3, 1, 2)).reshape(3 * chans, 3 * chans)
    w_up = jnp.transpose(w_time, (2, 0, 1)).reshape(chans, 3 * chans)
    w_both = jnp.concatenate([jnp.pad(w_up, ((0, 0), (f * chans, (nf - 1 - f) * chans))) for f in range(nf)], axis=0)
    x3, act, slope, edge_slope = call(
        forward_kernel,
        (field, from_left, from_right, own, w_fwd),
        (
            shape((nf, rows, 3 * chans, cols), BF16),
            shape((nf,) + slabs, BF16),
            shape((nf,) + slabs, F32),
            shape((chans, cols), F32),
        ),
        [pltpu.VMEM((rows + 2, 3 * chans, cols), F32)],
        10_000_000,
    )
    dpre, total = call(
        grads_kernel,
        (cot, later, act, slope, x3, w_both),
        (shape((nf,) + slabs, BF16), sums),
        [pltpu.VMEM((nf, rows + 2, chans, cols), BF16)],
        4_000_000_000,
    )
    total, near, far, w_bwd = lax.optimization_barrier((total, near, far, w_bwd))
    (out,) = call(
        back_kernel,
        (dpre, near, far, edge_slope, w_up, w_bwd),
        (shape((nf,) + slabs, BF16),),
        [pltpu.VMEM((rows + 2, 3 * chans, cols), F32)],
        4_000_000_000,
    )
    grad_frames = with_layout_constraint(jnp.transpose(out, (2, 0, 1, 3)), Layout(major_to_minor=(0, 1, 2, 3)))
    cells = nf * lax.axis_size(TM) * rows * cols * lax.axis_size(LON)
    total, grad_frames = sum_over_all(total.reshape(-1, 2 * chans), grad_frames)
    total = total.reshape(sums.shape)
    grad_sp, grad_tm = call(
        functools.partial(finish_kernel, 1.0 / math.sqrt(cells)),
        (total,),
        (shape(w_space.shape, F32), shape(w_time.shape, F32)),
        [],
        1_000_000,
    )
    return grad_frames, grad_sp, grad_tm


def solution(mesh):
    fine = Mesh(np.asarray(mesh.devices).reshape(4, 2, 2, 8, 2), AXES)
    field = P(None, TM, None, LON)
    return jax.shard_map(
        body,
        mesh=fine,
        in_specs=(field, field, P(), P()),
        out_specs=(field, P(), P()),
        check_vma=False,
    )
```

```python
import functools
import math

import jax
import jax.numpy as jnp
import numpy as np
from jax import lax
from jax.experimental import pallas as pl
from jax.experimental.layout import Layout, with_layout_constraint
from jax.experimental.pallas import tpu as pltpu
from jax.sharding import Mesh
from jax.sharding import PartitionSpec as P

AXES = ("y", "xh", "xl", "z", "c")
TM = ("y", "xh")
LON = ("xl", "z", "c")
PLANE = ("y", "xh", "xl")
F32 = jnp.float32
BF16 = jnp.bfloat16
ROWS = 8
GAP = 32
VMEM_LIMIT = 16 * 1024 * 1024


def dot_nt(a, b):
    return lax.dot_general(a, b, (((1,), (1,)), ((), ())), preferred_element_type=F32)


def lane_of(f, h):
    return 2 * (f * GAP + h)


def lane_taps(slab, edge, at):
    width = slab.shape[1]
    lane = lax.broadcasted_iota(jnp.int32, slab.shape, 1)
    wide = slab.astype(F32)
    beside = pltpu.roll(edge, width - 1 - at, 1)
    before = jnp.where(lane == 0, beside, pltpu.roll(wide, 1, 1))
    after = jnp.where(lane == width - 1, beside, pltpu.roll(wide, width - 1, 1))
    return before.astype(BF16), slab, after.astype(BF16)


def edge_kernel(x_ref, c_ref, right_ref, left_ref, own_ref):
    frames, rows, chans, cols = x_ref.shape
    lane = lax.broadcasted_iota(jnp.int32, (chans, cols), 1)
    sums = (jnp.zeros((chans, cols), F32),) * 6
    for f in range(frames):

        def step(g, sums, f=f):
            for r in range(ROWS):
                h = g * ROWS + r
                at = lane_of(f, h)
                right, left, past = (lane == at + k for k in range(3))
                wide = x_ref[f, h].astype(F32)
                low = pltpu.roll(wide, at, 1)
                high = pltpu.roll(wide, at + 3, 1)
                cot = c_ref[f * rows + h].astype(F32)
                vals = (low, low, high, high, pltpu.roll(cot, at, 1), pltpu.roll(cot, at + 2, 1))
                masks = (right, left, left, past, right, left)
                sums = tuple(jnp.where(m, v, s) for m, v, s in zip(masks, vals, sums))
            return sums

        sums = lax.fori_loop(0, rows // ROWS, step, sums)
    first, second, before_last, last, cot_first, cot_last = sums
    second, last = (pltpu.roll(cells, cols - 1, 1) for cells in (second, last))
    for ref, cells in ((right_ref, (before_last, last, cot_last)), (left_ref, (first, second, cot_first))):
        for i, part in enumerate(cells):
            ref[i * chans : (i + 1) * chans] = part.astype(BF16)
    own_ref[...] = (pltpu.roll(first, 1, 1) + pltpu.roll(last, cols - 1, 1)).astype(BF16)


def silu_parts(pre):
    s = 1.0 / (1.0 + jnp.exp(-pre))
    return pre * s, s * (1.0 + pre * (1.0 - s))


def forward_kernel(x_ref, from_left_ref, from_right_ref, own_ref, w_ref, x3_ref, act_ref, slope_ref, edge_slope_ref, y_ref):
    frames, rows, chans, cols = x_ref.shape
    weight = w_ref[...]
    left = lax.broadcasted_iota(jnp.int32, (chans, cols), 1) % 2 == 1
    own = own_ref[...].astype(F32)
    taps = [
        jnp.where(left, a.astype(F32), b.astype(F32))
        for a, b in (
            (from_left_ref[0:chans], own),
            (from_left_ref[chans : 2 * chans], from_right_ref[0:chans]),
            (own, from_right_ref[chans : 2 * chans]),
        )
    ]
    edge = taps[1]
    ye = jnp.dot(weight, jnp.concatenate(taps, axis=0).astype(BF16), preferred_element_type=F32)
    pre = (
        pltpu.roll(ye[0:chans], 2, 1)
        + ye[chans : 2 * chans]
        + pltpu.roll(ye[2 * chans : 3 * chans], cols - 2, 1)
    )
    edge_slope_ref[...] = silu_parts(pre)[1]
    zero = jnp.zeros((3 * chans, cols), F32)
    y_ref[0] = zero
    y_ref[rows + 1] = zero
    for f in range(frames):

        @pl.loop(0, rows // ROWS)
        def _(g):
            wide = []
            for r in range(ROWS):
                h = g * ROWS + r
                x3 = jnp.concatenate(lane_taps(x_ref[f, h], edge, lane_of(f, h)), axis=0)
                x3_ref[f, h] = x3
                wide.append(x3)
            y = jnp.dot(weight, jnp.concatenate(wide, axis=1), preferred_element_type=F32)
            for r in range(ROWS):
                y_ref[g * ROWS + r + 1] = y[:, r * cols : (r + 1) * cols]

        @pl.loop(0, rows // ROWS)
        def _(g):
            for r in range(ROWS):
                h = g * ROWS + r
                pre = (
                    y_ref[h, 0:chans]
                    + y_ref[h + 1, chans : 2 * chans]
                    + y_ref[h + 2, 2 * chans : 3 * chans]
                )
                act, slope = silu_parts(pre)
                act_ref[f, h] = act.astype(BF16)
                slope_ref[f, h] = slope


def grads_kernel(c_ref, later_ref, act_ref, slope_ref, x3_ref, w_ref, d_ref, sum_ref, d_scr):
    frames, rows, chans, cols = d_ref.shape
    weight = w_ref[...]
    wide = lambda ref, f, hs: jnp.concatenate([ref[f, h] for h in hs], axis=1)
    for f in range(frames):
        d_scr[f, 0] = jnp.zeros((chans, cols), BF16)
        d_scr[f, rows + 1] = jnp.zeros((chans, cols), BF16)
    t_sum = jnp.zeros((2 * frames * chans, frames * chans), F32)
    for g in range(rows // ROWS):
        hs = range(g * ROWS, (g + 1) * ROWS)
        cot = jnp.concatenate(
            [
                jnp.concatenate([ref[f * rows + h] for h in hs], axis=1)
                for ref in (c_ref, later_ref)
                for f in range(frames)
            ],
            axis=0,
        )
        up = jnp.dot(weight, cot, preferred_element_type=F32)
        for f in range(frames):
            for r, h in enumerate(hs):
                d = (up[f * chans : (f + 1) * chans, r * cols : (r + 1) * cols] * slope_ref[f, h]).astype(BF16)
                d_ref[f, h] = d
                d_scr[f, h + 1] = d
        t_sum = t_sum + dot_nt(cot, jnp.concatenate([wide(act_ref, f, hs) for f in range(frames)], axis=0))
    g_sum = jnp.zeros((3 * chans, 3 * chans), F32)
    for f in range(frames):
        for g in range(rows // ROWS):
            hs = range(g * ROWS, (g + 1) * ROWS)
            d3 = jnp.concatenate(
                [jnp.concatenate([d_scr[f, h - i + 2] for h in hs], axis=1) for i in range(3)], axis=0
            )
            g_sum = g_sum + dot_nt(d3, wide(x3_ref, f, hs))
    t_sum = t_sum[: 3 * chans, :chans] + t_sum[chans:, chans:]
    both = jnp.concatenate([g_sum, t_sum], axis=1)
    half = both.shape[1] // 2
    sum_ref[0] = both[:, :half]
    sum_ref[1] = both[:, half:]


def back_kernel(d_ref, near_ref, far_ref, slope_ref, w_up_ref, w_ref, out_ref, z_ref):
    frames, rows, chans, cols = d_ref.shape
    weight = w_ref[...]
    lane = lax.broadcasted_iota(jnp.int32, (chans, cols), 1)
    near = near_ref[...].astype(F32)
    far = far_ref[...].astype(F32)
    mixed = jnp.where(lane < 2 * GAP, pltpu.roll(near, cols - 2 * GAP, 1), pltpu.roll(far, 2 * GAP, 1))
    cot = jnp.concatenate([near, mixed, far], axis=0).astype(BF16)
    up = jnp.dot(w_up_ref[...], cot, preferred_element_type=F32)
    edge = (up * slope_ref[...]).astype(BF16).astype(F32)
    zero = jnp.zeros((3 * chans, cols), F32)
    z_ref[0] = zero
    z_ref[rows + 1] = zero
    for f in range(frames):

        @pl.loop(0, rows // ROWS)
        def _(g):
            wide = []
            for r in range(ROWS):
                h = g * ROWS + r
                before, same, after = lane_taps(d_ref[f, h], edge, lane_of(f, h))
                wide.append(jnp.concatenate([after, same, before], axis=0))
            z = jnp.dot(weight, jnp.concatenate(wide, axis=1), preferred_element_type=F32)
            for r in range(ROWS):
                z_ref[g * ROWS + r + 1] = z[:, r * cols : (r + 1) * cols]

        @pl.loop(0, rows // ROWS)
        def _(g):
            for r in range(ROWS):
                h = g * ROWS + r
                out = (
                    z_ref[h + 2, 0:chans]
                    + z_ref[h + 1, chans : 2 * chans]
                    + z_ref[h, 2 * chans : 3 * chans]
                )
                out_ref[f, h] = out.astype(BF16)


def finish_kernel(scale, sum_ref, space_ref, time_ref):
    taps, chans = time_ref.shape[:2]
    for i in range(taps):
        rows = slice(i * chans, (i + 1) * chans)
        low = sum_ref[0, rows, :].astype(F32) * scale
        high = sum_ref[1, rows, :].astype(F32) * scale
        space_ref[i, 0] = low[:, :chans]
        space_ref[i, 1] = low[:, chans:]
        space_ref[i, 2] = high[:, :chans]
        time_ref[i] = high[:, chans:]


def in_vmem(count):
    return [pl.BlockSpec(memory_space=pltpu.VMEM)] * count


def call(kernel, args, outs, scratch, flops):
    return pl.pallas_call(
        kernel,
        out_shape=outs,
        in_specs=in_vmem(len(args)),
        out_specs=tuple(in_vmem(len(outs))),
        scratch_shapes=scratch,
        compiler_params=pltpu.CompilerParams(vmem_limit_bytes=VMEM_LIMIT),
        cost_estimate=pl.CostEstimate(flops=flops, transcendentals=0, bytes_accessed=flops // 1000),
    )(*args)


def exchange(cells, axes):
    return lax.all_to_all(cells, axes, 0, 0, tiled=True)


def spread(cells, axes):
    count = lax.axis_size(axes)
    return exchange(jnp.broadcast_to(cells[None], (count,) + cells.shape), axes)


def sum_over_all(cells, beside):
    count = lax.axis_size(PLANE)
    parts = exchange(cells.reshape(count, -1, cells.shape[-1]), PLANE).sum(0)
    parts = parts + lax.ppermute(parts, "c", [(0, 1), (1, 0)])
    parts, beside = lax.optimization_barrier((spread(parts, "z"), beside))
    parts = parts.sum(0)
    return spread(parts.astype(BF16), PLANE).reshape(cells.shape), beside


def shifted(cells, tm_step, lon_step):
    blocks, sectors = lax.axis_size(TM), lax.axis_size(LON)
    pairs = [
        ((t + tm_step) % blocks * sectors + (s + lon_step) % sectors, t * sectors + s)
        for t in range(blocks)
        for s in range(sectors)
    ]
    return lax.ppermute(cells, TM + LON, pairs)


def body(frames, cotangent, w_space, w_time):
    chans, nf, rows, cols = frames.shape
    shape = jax.ShapeDtypeStruct
    slabs = (rows, chans, cols)
    edge = shape((chans, cols), BF16)
    edges = shape((3 * chans, cols), BF16)
    sums = shape((2, 3 * chans, 2 * chans), F32)
    by_row = lambda field: jnp.transpose(field, (1, 2, 0, 3)).reshape(nf * rows, chans, cols)
    keep = (lax.axis_index(TM) < lax.axis_size(TM) - 1).astype(BF16)
    later = by_row(shifted(cotangent, 1, 0)) * keep
    cot, field = by_row(cotangent), jnp.transpose(frames, (1, 2, 0, 3))
    to_right, to_left, own = call(edge_kernel, (field, cot), (edges, edges, edge), [], 10_000_000)
    from_left, from_right = shifted(to_right, 0, -1), shifted(to_left, 0, 1)
    near = from_left[2 * chans :] + from_right[2 * chans :]
    far = shifted(near, 1, 0) * keep
    w_fwd = jnp.transpose(w_space, (0, 2, 1, 3)).reshape(3 * chans, 3 * chans)
    w_bwd = jnp.transpose(w_space, (0, 3, 1, 2)).reshape(3 * chans, 3 * chans)
    w_up = jnp.transpose(w_time, (2, 0, 1)).reshape(chans, 3 * chans)
    w_both = jnp.concatenate([jnp.pad(w_up, ((0, 0), (f * chans, (nf - 1 - f) * chans))) for f in range(nf)], axis=0)
    x3, act, slope, edge_slope = call(
        forward_kernel,
        (field, from_left, from_right, own, w_fwd),
        (
            shape((nf, rows, 3 * chans, cols), BF16),
            shape((nf,) + slabs, BF16),
            shape((nf,) + slabs, F32),
            shape((chans, cols), F32),
        ),
        [pltpu.VMEM((rows + 2, 3 * chans, cols), F32)],
        10_000_000,
    )
    dpre, total = call(
        grads_kernel,
        (cot, later, act, slope, x3, w_both),
        (shape((nf,) + slabs, BF16), sums),
        [pltpu.VMEM((nf, rows + 2, chans, cols), BF16)],
        4_000_000_000,
    )
    total, near, far, w_bwd = lax.optimization_barrier((total, near, far, w_bwd))
    (out,) = call(
        back_kernel,
        (dpre, near, far, edge_slope, w_up, w_bwd),
        (shape((nf,) + slabs, BF16),),
        [pltpu.VMEM((rows + 2, 3 * chans, cols), F32)],
        4_000_000_000,
    )
    grad_frames = with_layout_constraint(jnp.transpose(out, (2, 0, 1, 3)), Layout(major_to_minor=(0, 1, 2, 3)))
    cells = nf * lax.axis_size(TM) * rows * cols * lax.axis_size(LON)
    total, grad_frames = sum_over_all(total.reshape(-1, 2 * chans), grad_frames)
    total = total.reshape(sums.shape)
    grad_sp, grad_tm = call(
        functools.partial(finish_kernel, 1.0 / math.sqrt(cells)),
        (total,),
        (shape(w_space.shape, F32), shape(w_time.shape, F32)),
        [],
        1_000_000,
    )
    return grad_frames, grad_sp, grad_tm


def solution(mesh):
    fine = Mesh(np.asarray(mesh.devices).reshape(4, 2, 2, 8, 2), AXES)
    field = P(None, TM, None, LON)
    return jax.shard_map(
        body,
        mesh=fine,
        in_specs=(field, field, P(), P()),
        out_specs=(field, P(), P()),
        check_vma=False,
    )
```
